768 devices in a mesh: rep: 192 (over z, x, y_lo, core), shard: 4 (over y_hi).
Axes of the slice: x: 4, y: 8 (y_hi: 4, y_lo: 2; y = y_hi * 2 + y_lo), z: 12, core: 2. Of those that a mesh axis runs over, the one named last changes fastest.
Arguments:
- activations: bfloat16 [24576, 1984], P('rep'), may hold values from -6 to 6
- out_grads: bfloat16 [24576, 992], P('rep', 'shard'), may hold values from -1.5 to 1.5
- error: bfloat16 [192, 1984, 992], P('rep', None, 'shard'), may hold values from -12 to 12
- momentum: bfloat16 [1984, 992], P(None, 'shard'), may hold values from -1.1953125 to 1.1953125
- query: float32 [992, 64], P('shard'), may hold values from -6 to 6
Outputs:
- error_new: bfloat16 [192, 1984, 992], P('rep', None, 'shard')
- momentum_new: bfloat16 [1984, 992], P(None, 'shard')
- query_new: float32 [992, 64], P('shard')
The draws below stay inside these ranges and needn't reach their ends.
All inputs are finite; a program needn't handle non-finite values.
Results may differ from the reference program's by a relative error of at most 0.001.
Values sent between devices are 32-bit elements; how exact they have to be, the bound alone decides.
No kernel may reach another device: no remote copies, remote signals or barrier semaphores. Data moves between devices by JAX's collectives and lax.ppermute only.
A program may use at most 32 MiB of HBM per device.

```python
import jax
import jax.numpy as jnp
from jax import lax

D = 1984
RANK = 64
TOK_DEV = 128
TOKENS = 24576
COLS = 992
N_REP = 192


def block_scale(own_key, extent, shards, smallest, top_value):
    factor_of, own = 1.0, jax.random.fold_in(own_key, 6)
    for axis_at, blocks in shards:
        steps = jnp.exp(jax.random.uniform(jax.random.fold_in(own, axis_at), (blocks,), jnp.float32, smallest / len(shards), top_value / len(shards)))
        factor_of = factor_of * jnp.repeat(steps, extent[axis_at] // blocks).reshape([-1 if axis == axis_at else 1 for axis in range(len(extent))])
    return factor_of


def normal_values(key, extent, deviation, bound, pieces=(), kind=jnp.bfloat16):
    entries = deviation * jax.random.normal(key, extent, jnp.float32)
    if pieces:
        entries = entries * block_scale(key, extent, pieces, -0.22, 0.18)
    return jnp.clip(entries, -bound, bound).astype(kind)


def setup_inputs(seed: int = 0) -> dict:
    splits = jax.random.split(jax.random.key(seed), 6)
    activations = normal_values(splits[0], (TOKENS, D), 1.0, 6.0, ((0, 192),))
    out_grads = normal_values(splits[1], (TOKENS, COLS), 0.25, 1.5, ((0, 192), (1, 4)))
    error = normal_values(splits[2], (N_REP, D, COLS), 2.0, 12.0, ((0, 192), (2, 4)))
    momentum = normal_values(splits[3], (D, COLS), 0.2, 1.1953125, ((1, 4),))
    query = normal_values(splits[4], (COLS, RANK), 1.0, 6.0, ((0, 4),), jnp.float32)
    return {"activations": activations, "out_grads": out_grads, "error": error, "momentum": momentum, "query": query}


def merged_block(act_rows, grad_rows, err_block):
    grad = jnp.dot(act_rows.T.astype(jnp.float32), grad_rows.astype(jnp.float32), preferred_element_type=jnp.float32)
    return grad + err_block.astype(jnp.float32)

def reference(activations, out_grads, error, momentum, query):
    acts = activations.reshape(N_REP, TOK_DEV, D)
    grads = out_grads.reshape(N_REP, TOK_DEV, COLS)
    steps_idx = jnp.arange(N_REP).astype(jnp.int32)

    def add_factor(total, index):
        merged = merged_block(acts[index], grads[index], error[index])
        return (total + jnp.dot(merged, query, precision=lax.Precision.HIGHEST), None)
    factor, unused = lax.scan(add_factor, jnp.zeros((D, RANK), jnp.float32), steps_idx)
    gram = jnp.dot(factor.T, factor, precision=lax.Precision.HIGHEST)
    lower = jnp.linalg.cholesky(gram)
    basis = jax.scipy.linalg.solve_triangular(lower, factor.T, lower=True).T

    def add_query(total, index):
        merged = merged_block(acts[index], grads[index], error[index])
        return (total + jnp.dot(merged.T, basis, precision=lax.Precision.HIGHEST), None)
    qsum, unused = lax.scan(add_query, jnp.zeros((COLS, RANK), jnp.float32), steps_idx)
    query_new = qsum / N_REP
    approx = jnp.dot(basis, query_new.T, precision=lax.Precision.HIGHEST)

    def new_error(index):
        merged = merged_block(acts[index], grads[index], error[index])
        return (merged - approx).astype(jnp.bfloat16)
    error_new = lax.map(new_error, steps_idx)
    momentum_new = (0.9 * momentum.astype(jnp.float32) + approx).astype(jnp.bfloat16)
    return (error_new, momentum_new, query_new)
```

```python
import jax
import jax.numpy as jnp
from jax import lax
from jax.sharding import Mesh, PartitionSpec as P

HIGHEST = lax.Precision.HIGHEST
BLOCKS, BLOCK = 8, 256
XC = ("x", "c")
Y = ("yl", "yh")
XYC = ("x", "yl", "c")
Z = "z"


def exchange(pieces, axes):
    return lax.all_to_all(pieces, axes, 0, 0)


def scatter_sum(pieces, axes):
    return jnp.sum(exchange(pieces, axes), 0)


def gather(piece, axes):
    copies = jnp.broadcast_to(piece[None], (lax.axis_size(axes), *piece.shape))
    return exchange(copies, axes)


def gather_sum(piece, axes):
    return jnp.sum(gather(piece, axes), 0)


def shards(activations, out_grads, error, momentum, query):
    rows, cols = error.shape[1:]
    rank = query.shape[1]
    grad = lax.dot_general(
        activations, out_grads, (((0,), (0,)), ((), ())), preferred_element_type=jnp.float32
    )
    merged = grad + error[0].astype(jnp.float32)
    padded = jnp.pad(merged, ((0, BLOCKS * BLOCK - rows), (0, 0))).reshape(BLOCKS, BLOCK, cols)
    partial = jnp.einsum("bdc,ck->bkd", padded, query, precision=HIGHEST)

    piece = scatter_sum(partial, XC)
    piece = scatter_sum(piece.reshape(8, rank // 8, BLOCK), Y)
    piece = gather_sum(piece, Z)
    piece = gather(piece, Y).reshape(rank, BLOCK)
    factor = gather(piece, XC)

    gram = jnp.einsum("bkd,bld->kl", factor, factor, precision=HIGHEST)
    lower = jnp.linalg.cholesky(gram)
    inverse = jax.scipy.linalg.solve_triangular(lower, jnp.eye(rank, dtype=jnp.float32), lower=True)

    local = jnp.einsum("bkd,bdc->kc", factor, padded, precision=HIGHEST)
    local = jnp.pad(local, ((0, 0), (0, 256 - cols)))
    tiles = local.reshape(8, 8, 2, 128).transpose(0, 2, 1, 3).reshape(16, 8, 128)
    piece = scatter_sum(tiles, XYC)
    piece = gather_sum(piece, Z)
    tiles = gather(piece, XYC)
    total = tiles.reshape(8, 2, 8, 128).transpose(0, 2, 1, 3).reshape(rank, 256)[:, :cols]

    replicas = lax.axis_size((Z, *XYC))
    query_t = jnp.dot(inverse, total, precision=HIGHEST) / replicas
    weights = jnp.dot(inverse.T, query_t, precision=HIGHEST)
    approx = jnp.einsum("bkd,kc->bdc", factor, weights, precision=HIGHEST)
    approx = approx.reshape(BLOCKS * BLOCK, cols)[:rows]
    error_new = (merged - approx).astype(jnp.bfloat16)[None]
    momentum_new = (0.9 * momentum.astype(jnp.float32) + approx).astype(jnp.bfloat16)
    return (error_new, momentum_new, query_t.T)


def solution(mesh):
    fine = Mesh(mesh.devices.reshape(12, 4, 2, 2, 4), ("z", "x", "yl", "c", "yh"))
    rep, shard = ("z", "x", "yl", "c"), "yh"
    return jax.shard_map(
        shards,
        mesh=fine,
        in_specs=(
            P(rep, None),
            P(rep, shard),
            P(rep, None, shard),
            P(None, shard),
            P(shard, None),
        ),
        out_specs=(P(rep, None, shard), P(None, shard), P(shard, None)),
        check_vma=False,
    )
```

```python
import jax
import jax.numpy as jnp
from jax import lax
from jax.experimental import pallas as pl
from jax.experimental.pallas import tpu as pltpu
from jax.sharding import Mesh, PartitionSpec as P

F32, BF16 = jnp.float32, jnp.bfloat16
BLOCKS, GROUP, LANES = 8, 2, 256
XC = ("x", "c")
Y = ("yl", "yh")
XYC = ("x", "yl", "c")
Z = "z"
NN = (((1,), (0,)), ((), ()))
NT = (((1,), (1,)), ((), ()))
TN = (((0,), (0,)), ((), ()))


def in_hbm(value):
    return pltpu.with_memory_space_constraint(value, pltpu.HBM)


def params(mib):
    return pltpu.CompilerParams(vmem_limit_bytes=mib << 20)


def cost(flops, size):
    return pl.CostEstimate(flops=flops, bytes_accessed=size, transcendentals=0)


def split(value):
    high = value.astype(BF16)
    return high, (value - high.astype(F32)).astype(BF16)


def dot(left, right, dims):
    return lax.dot_general(left, right, dims, preferred_element_type=F32)


def dot_split(left, right, dims):
    (lh, ll), (rh, rl) = left, right
    return dot(lh, rh, dims) + (dot(lh, rl, dims) + dot(ll, rh, dims))


def dot_full(left, right, dims):
    return lax.dot_general(
        left, right, dims, precision=lax.Precision.HIGHEST, preferred_element_type=F32
    )


def merge_kernel(act_ref, grad_ref, err_ref, query_ref, merged_ref, partial_ref):
    query = split(query_ref[...])
    for i in range(GROUP):
        merged = dot(act_ref[i], grad_ref[...], NT) + err_ref[i].astype(F32)
        merged_ref[i] = merged
        rows = merged.shape[0]
        partial_ref[i, :, :rows] = dot_split(query, split(merged), NT)
        partial_ref[i, :, rows:] = jnp.zeros((partial_ref.shape[1], LANES - rows), F32)


def merge(act, grad, err, query):
    blocks, rows, cols = err.shape
    tok, rank = act.shape[2], query.shape[0]
    return pl.pallas_call(
        merge_kernel,
        grid=(blocks // GROUP,),
        in_specs=[
            pl.BlockSpec((GROUP, rows, tok), lambda i: (i, 0, 0)),
            pl.BlockSpec((cols, tok), lambda i: (0, 0)),
            pl.BlockSpec((GROUP, rows, cols), lambda i: (i, 0, 0)),
            pl.BlockSpec((rank, cols), lambda i: (0, 0)),
        ],
        out_specs=[
            pl.BlockSpec((GROUP, rows, cols), lambda i: (i, 0, 0)),
            pl.BlockSpec((GROUP, rank, LANES), lambda i: (i, 0, 0)),
        ],
        out_shape=[
            jax.ShapeDtypeStruct((blocks, rows, cols), F32),
            jax.ShapeDtypeStruct((blocks, rank, LANES), F32),
        ],
        compiler_params=params(16),
        cost_estimate=cost(500_000_000, 4 << 20),
        name="merge",
    )(act, grad, err, query)


def project_kernel(factor_ref, merged_ref, tiles_ref, total):
    step = pl.program_id(0)
    rows, cols = merged_ref.shape[1:]
    value = jnp.zeros((factor_ref.shape[1], cols), F32)
    for i in range(GROUP):
        factor = factor_ref[i][:, :rows]
        value += dot_split(split(factor), split(merged_ref[i]), NN)

    @pl.when(step == 0)
    def _():
        total[...] = jnp.zeros_like(total)

    total[:, :cols] += value

    @pl.when(step == pl.num_programs(0) - 1)
    def _():
        for j in range(tiles_ref.shape[0]):
            r, c = divmod(j, 2)
            tiles_ref[j] = total[8 * r : 8 * r + 8, 128 * c : 128 * c + 128]


def project(factor, merged):
    blocks, rows, cols = merged.shape
    rank = factor.shape[1]
    tiles = rank * LANES // 1024
    return pl.pallas_call(
        project_kernel,
        grid=(blocks // GROUP,),
        in_specs=[
            pl.BlockSpec((GROUP, rank, LANES), lambda i: (i, 0, 0)),
            pl.BlockSpec((GROUP, rows, cols), lambda i: (i, 0, 0)),
        ],
        out_specs=pl.BlockSpec((tiles, 8, 128), lambda i: (0, 0, 0)),
        out_shape=jax.ShapeDtypeStruct((tiles, 8, 128), F32),
        scratch_shapes=[pltpu.VMEM((rank, LANES), F32)],
        compiler_params=params(16),
        cost_estimate=cost(400_000_000, 3 << 20),
        name="project",
    )(factor, merged)


def invert_kernel(replicas, factor_ref, inverse_ref, weights_ref):
    blocks, rank = factor_ref.shape[:2]
    gram = jnp.zeros((rank, rank), F32)
    for b in range(blocks):
        gram += dot_full(factor_ref[b], factor_ref[b], NT)
    lane = lax.broadcasted_iota(jnp.int32, (rank, rank), 1)
    eye = (lane == lax.broadcasted_iota(jnp.int32, (rank, rank), 0)).astype(F32)
    wide = jnp.concatenate([gram, eye], axis=1)
    tiles = [wide[8 * t : 8 * t + 8] for t in range(rank // 8)]
    sub = lax.broadcasted_iota(jnp.int32, (8, 1), 0)
    for k in range(rank):
        at, r = divmod(k, 8)
        row = tiles[at][r : r + 1]
        scaled = row * (1.0 / row[:, k : k + 1])
        for t in range(at, len(tiles)):
            column = tiles[t][:, k : k + 1]
            if t == at:
                column = jnp.where(sub > r, column, 0.0)
            tiles[t] = tiles[t] - column * scaled
    wide = jnp.concatenate(tiles, axis=0)
    pivots = jnp.sum(wide[:, :rank] * eye, axis=1, keepdims=True)
    inverse = wide[:, rank:] / jnp.sqrt(pivots)
    inverse_ref[...] = inverse / replicas
    weights_ref[...] = dot_full(inverse, inverse, TN) / replicas


def invert(factor, replicas):
    rank = factor.shape[1]
    square = jax.ShapeDtypeStruct((rank, rank), F32)
    return pl.pallas_call(
        lambda *refs: invert_kernel(replicas, *refs),
        out_shape=[square, square],
        compiler_params=params(16),
        cost_estimate=cost(7_000_000_000, 1 << 20),
        name="invert",
    )(factor)


def spread_kernel(factor_ref, weights_ref, left_ref):
    blocks, rows = left_ref.shape[:2]
    for b in range(blocks):
        left = split(dot_full(factor_ref[b], weights_ref[...], TN)[:rows])
        left_ref[b] = jnp.concatenate(left, axis=1)


def spread(factor, weights, rows):
    blocks, rank = factor.shape[:2]
    return pl.pallas_call(
        spread_kernel,
        out_shape=jax.ShapeDtypeStruct((blocks, rows, 2 * rank), BF16),
        compiler_params=params(16),
        cost_estimate=cost(2_000_000_000, 1 << 20),
        name="spread",
    )(factor, weights)


def finish_kernel(inverse_ref, tiles_ref, left_ref, merged_ref, mom_ref,
                  error_ref, momentum_ref, query_ref, total):
    rank, cols = query_ref.shape

    @pl.when(pl.program_id(0) == 0)
    def _():
        for j in range(tiles_ref.shape[0]):
            r, c = divmod(j, 2)
            total[8 * r : 8 * r + 8, 128 * c : 128 * c + 128] = tiles_ref[j]
        query_ref[...] = dot_full(inverse_ref[...], total[...], NN)[:, :cols]

    high, low = split(total[...])
    both = jnp.concatenate([high, high], axis=0)
    rest = jnp.concatenate([low, jnp.zeros_like(low)], axis=0)
    for i in range(GROUP):
        approx = (dot(left_ref[i], both, NN) + dot(left_ref[i], rest, NN))[:, :cols]
        error_ref[i] = (merged_ref[i] - approx).astype(BF16)
        momentum_ref[i] = (0.9 * mom_ref[i].astype(F32) + approx).astype(BF16)


def finish(inverse, tiles, left, merged, momentum):
    blocks, rows, cols = merged.shape
    rank = inverse.shape[0]
    block = pl.BlockSpec((GROUP, rows, cols), lambda i: (i, 0, 0))
    out = jax.ShapeDtypeStruct((blocks, rows, cols), BF16)
    return pl.pallas_call(
        finish_kernel,
        grid=(blocks // GROUP,),
        in_specs=[
            pl.BlockSpec((rank, rank), lambda i: (0, 0)),
            pl.BlockSpec(tiles.shape, lambda i: (0, 0, 0)),
            pl.BlockSpec((GROUP, rows, 2 * rank), lambda i: (i, 0, 0)),
            block,
            block,
        ],
        out_specs=[block, block, pl.BlockSpec((rank, cols), lambda i: (0, 0))],
        out_shape=[out, out, jax.ShapeDtypeStruct((rank, cols), F32)],
        scratch_shapes=[pltpu.VMEM((rank, LANES), F32)],
        compiler_params=params(16),
        cost_estimate=cost(400_000_000, 6 << 20),
        name="finish",
    )(inverse, tiles, left, merged, momentum)


def exchange(pieces, axes):
    return lax.all_to_all(pieces, axes, 0, 0)


def scatter_sum(pieces, axes):
    return jnp.sum(exchange(pieces, axes), 0)


def gather(piece, axes):
    copies = jnp.broadcast_to(piece[None], (lax.axis_size(axes), *piece.shape))
    return exchange(copies, axes)


def gather_sum(piece, axes):
    return jnp.sum(gather(piece, axes), 0)


def shards(activations, out_grads, error, momentum, query):
    rows, cols = error.shape[1:]
    rank = query.shape[1]
    block = rows // BLOCKS
    merged, partial = merge(
        in_hbm(activations.T.reshape(BLOCKS, block, -1)),
        in_hbm(out_grads.T),
        in_hbm(error.reshape(BLOCKS, block, cols)),
        in_hbm(query.T),
    )
    piece = scatter_sum(partial, XC)
    piece = scatter_sum(piece.reshape(8, rank // 8, LANES), Y)
    piece = gather_sum(piece, Z)
    piece = gather(piece, Y).reshape(rank, LANES)
    factor = gather(piece, XC)

    piece = scatter_sum(project(factor, merged), XYC)
    piece, factor = lax.optimization_barrier((piece, factor))
    inverse, weights = invert(factor, lax.axis_size((Z, *XYC)))
    piece = gather_sum(piece, Z)
    piece, weights = lax.optimization_barrier((piece, weights))
    left = spread(factor, weights, block)
    tiles = gather(piece, XYC)
    error_new, momentum_new, query_t = finish(
        inverse, tiles, left, merged, in_hbm(momentum.reshape(BLOCKS, block, cols))
    )
    return (error_new.reshape(error.shape), momentum_new.reshape(momentum.shape), query_t.T)


def solution(mesh):
    fine = Mesh(mesh.devices.reshape(12, 4, 2, 2, 4), ("z", "x", "yl", "c", "yh"))
    rep, shard = ("z", "x", "yl", "c"), "yh"
    return jax.shard_map(
        shards,
        mesh=fine,
        in_specs=(
            P(rep, None),
            P(rep, shard),
            P(rep, None, shard),
            P(None, shard),
            P(shard, None),
        ),
        out_specs=(P(rep, None, shard), P(None, shard), P(shard, None)),
        check_vma=False,
    )
```

```python
import jax
import jax.numpy as jnp
from jax import lax
from jax.experimental import pallas as pl
from jax.experimental.pallas import tpu as pltpu
from jax.sharding import Mesh, PartitionSpec as P

F32, BF16 = jnp.float32, jnp.bfloat16
BLOCKS, GROUP, LANES = 8, 4, 256
XC = ("x", "c")
Y = ("yl", "yh")
XYC = ("x", "yl", "c")
Z = "z"
NN = (((1,), (0,)), ((), ()))
NT = (((1,), (1,)), ((), ()))
TN = (((0,), (0,)), ((), ()))


def in_hbm(value):
    return pltpu.with_memory_space_constraint(value, pltpu.HBM)


def params(mib):
    return pltpu.CompilerParams(vmem_limit_bytes=mib << 20)


def cost(flops, size):
    return pl.CostEstimate(flops=flops, bytes_accessed=size, transcendentals=0)


def split(value):
    high = value.astype(BF16)
    return high, (value - high.astype(F32)).astype(BF16)


def dot(left, right, dims):
    return lax.dot_general(left, right, dims, preferred_element_type=F32)


def dot_split(left, right, dims):
    (lh, ll), (rh, rl) = left, right
    return dot(lh, rh, dims) + (dot(lh, rl, dims) + dot(ll, rh, dims))


def dot_full(left, right, dims):
    return lax.dot_general(
        left, right, dims, precision=lax.Precision.HIGHEST, preferred_element_type=F32
    )


def merge_kernel(act_hbm, grad_hbm, err_hbm, query_hbm, merged_ref, partial_ref,
                 act_ref, grad_ref, err_ref, query_ref, sems):
    blocks, rows = merged_ref.shape[:2]
    rank = partial_ref.shape[1]
    small = [
        pltpu.make_async_copy(grad_hbm, grad_ref, sems.at[0]),
        pltpu.make_async_copy(query_hbm, query_ref, sems.at[1]),
    ]
    large = []
    for g in range(0, blocks, GROUP):
        part = pl.ds(g, GROUP)
        large.append([
            pltpu.make_async_copy(act_hbm.at[part], act_ref.at[part], sems.at[2 + g]),
            pltpu.make_async_copy(err_hbm.at[part], err_ref.at[part], sems.at[3 + g]),
        ])
    for copy in [*small, *sum(large, [])]:
        copy.start()
    partial_ref[:, :, rows:] = jnp.zeros((blocks, rank, LANES - rows), F32)
    for copy in small:
        copy.wait()
    stacked = jnp.concatenate(split(query_ref[...]), axis=0)
    for b in range(blocks):
        if b % GROUP == 0:
            for copy in large[b // GROUP]:
                copy.wait()
        merged = dot(act_ref[b], grad_ref[...], NT) + err_ref[b].astype(F32)
        merged_ref[b] = merged
        high, low = split(merged)
        both = dot(stacked, high, NT)
        partial_ref[b, :, :rows] = both[:rank] + (both[rank:] + dot(stacked[:rank], low, NT))


def merge(act, grad, err, query):
    blocks, rows, cols = err.shape
    rank = query.shape[0]
    whole = pl.BlockSpec(memory_space=pltpu.VMEM)
    hbm = pl.BlockSpec(memory_space=pltpu.HBM)
    return pl.pallas_call(
        merge_kernel,
        in_specs=[hbm] * 4,
        out_specs=[whole] * 2,
        out_shape=[
            jax.ShapeDtypeStruct((blocks, rows, cols), F32),
            jax.ShapeDtypeStruct((blocks, rank, LANES), F32),
        ],
        scratch_shapes=[
            *(pltpu.VMEM(value.shape, value.dtype) for value in (act, grad, err, query)),
            pltpu.SemaphoreType.DMA((2 + blocks,)),
        ],
        compiler_params=params(16),
        cost_estimate=cost(500_000_000, 4 << 20),
        name="merge",
    )(act, grad, err, query)


def project_kernel(factor_ref, merged_ref, tiles_ref):
    blocks, rows, cols = merged_ref.shape
    rank = factor_ref.shape[1]
    both, rest = jnp.zeros((2 * rank, cols), F32), jnp.zeros((rank, cols), F32)
    for b in range(blocks):
        stacked = jnp.concatenate(split(factor_ref[b][:, :rows]), axis=0)
        high, low = split(merged_ref[b])
        both += dot(stacked, high, NN)
        rest += dot(stacked[:rank], low, NN)
    total = both[:rank] + (both[rank:] + rest)
    total = jnp.concatenate([total, jnp.zeros((rank, LANES - cols), F32)], axis=1)
    for j in range(tiles_ref.shape[0]):
        r, c = divmod(j, 2)
        tiles_ref[j] = total[8 * r : 8 * r + 8, 128 * c : 128 * c + 128]


def project(factor, merged):
    rank = factor.shape[1]
    whole = pl.BlockSpec(memory_space=pltpu.VMEM)
    return pl.pallas_call(
        project_kernel,
        in_specs=[whole] * 2,
        out_specs=whole,
        out_shape=jax.ShapeDtypeStruct((rank * LANES // 1024, 8, 128), F32),
        compiler_params=params(16),
        cost_estimate=cost(400_000_000, 3 << 20),
        name="project",
    )(factor, merged)


def invert_kernel(replicas, factor_ref, inverse_ref, weights_ref):
    blocks, rank = factor_ref.shape[:2]
    gram = jnp.zeros((rank, rank), F32)
    for b in range(blocks):
        gram += dot_full(factor_ref[b], factor_ref[b], NT)
    lane = lax.broadcasted_iota(jnp.int32, (rank, rank), 1)
    eye = (lane == lax.broadcasted_iota(jnp.int32, (rank, rank), 0)).astype(F32)
    wide = jnp.concatenate([gram, eye], axis=1)
    tiles = [wide[8 * t : 8 * t + 8] for t in range(rank // 8)]
    sub = lax.broadcasted_iota(jnp.int32, (8, 1), 0)
    for k in range(rank):
        at, r = divmod(k, 8)
        row = tiles[at][r : r + 1]
        scaled = row * (1.0 / row[:, k : k + 1])
        for t in range(at, len(tiles)):
            column = tiles[t][:, k : k + 1]
            if t == at:
                column = jnp.where(sub > r, column, 0.0)
            tiles[t] = tiles[t] - column * scaled
    wide = jnp.concatenate(tiles, axis=0)
    pivots = jnp.sum(wide[:, :rank] * eye, axis=1, keepdims=True)
    inverse = wide[:, rank:] / jnp.sqrt(pivots)
    inverse_ref[...] = inverse / replicas
    weights_ref[...] = dot_full(inverse, inverse, TN) / replicas


def invert(factor, replicas):
    rank = factor.shape[1]
    square = jax.ShapeDtypeStruct((rank, rank), F32)
    return pl.pallas_call(
        lambda *refs: invert_kernel(replicas, *refs),
        out_shape=[square, square],
        compiler_params=params(16),
        cost_estimate=cost(7_000_000_000, 1 << 20),
        name="invert",
    )(factor)


def spread_kernel(factor_ref, weights_ref, left_ref):
    blocks, rows = left_ref.shape[:2]
    for b in range(blocks):
        left = split(dot_full(factor_ref[b], weights_ref[...], TN)[:rows])
        left_ref[b] = jnp.concatenate(left, axis=1)


def spread(factor, weights, rows):
    blocks, rank = factor.shape[:2]
    return pl.pallas_call(
        spread_kernel,
        out_shape=jax.ShapeDtypeStruct((blocks, rows, 2 * rank), BF16),
        compiler_params=params(16),
        cost_estimate=cost(2_000_000_000, 1 << 20),
        name="spread",
    )(factor, weights)


def finish_kernel(inverse_ref, tiles_ref, left_ref, merged_ref, mom_hbm,
                  error_hbm, momentum_hbm, query_ref, mom_ref, error_ref, momentum_ref, sems):
    rank, cols = query_ref.shape
    blocks, rows = merged_ref.shape[:2]
    loads, stores = [], []
    for g in range(0, blocks, GROUP):
        part = pl.ds(g, GROUP)
        loads.append(pltpu.make_async_copy(mom_hbm.at[part], mom_ref.at[part], sems.at[0, g // GROUP]))
        stores.append([
            pltpu.make_async_copy(error_ref.at[part], error_hbm.at[part], sems.at[1, g // GROUP]),
            pltpu.make_async_copy(momentum_ref.at[part], momentum_hbm.at[part], sems.at[2, g // GROUP]),
        ])
    for copy in loads:
        copy.start()
    total = jnp.concatenate(
        [
            jnp.concatenate([tiles_ref[j], tiles_ref[j + 1]], axis=1)
            for j in range(0, tiles_ref.shape[0], 2)
        ],
        axis=0,
    )
    high, low = split(total)
    right = jnp.concatenate([high, high, low], axis=0)
    for b in range(blocks):
        left = left_ref[b]
        left = jnp.concatenate([left, left[:, :rank]], axis=1)
        approx = dot(left, right, NN)[:, :cols]
        if b % GROUP == 0:
            loads[b // GROUP].wait()
        error_ref[b] = (merged_ref[b] - approx).astype(BF16)
        momentum_ref[b] = (0.9 * mom_ref[b].astype(F32) + approx).astype(BF16)
        if b % GROUP == GROUP - 1:
            for copy in stores[b // GROUP]:
                copy.start()
    query_ref[...] = dot_full(inverse_ref[...], total, NN)[:, :cols]
    for pair in stores:
        for copy in pair:
            copy.wait()


def finish(inverse, tiles, left, merged, momentum):
    blocks, rows, cols = merged.shape
    rank = inverse.shape[0]
    whole = pl.BlockSpec(memory_space=pltpu.VMEM)
    hbm = pl.BlockSpec(memory_space=pltpu.HBM)
    out = jax.ShapeDtypeStruct((blocks, rows, cols), BF16)
    return pl.pallas_call(
        finish_kernel,
        in_specs=[whole, whole, whole, whole, hbm],
        out_specs=[hbm, hbm, whole],
        out_shape=[out, out, jax.ShapeDtypeStruct((rank, cols), F32)],
        scratch_shapes=[
            *(pltpu.VMEM((blocks, rows, cols), BF16) for _ in range(3)),
            pltpu.SemaphoreType.DMA((3, blocks // GROUP)),
        ],
        compiler_params=params(16),
        cost_estimate=cost(400_000_000, 6 << 20),
        name="finish",
    )(inverse, tiles, left, merged, momentum)


def exchange(pieces, axes):
    return lax.all_to_all(pieces, axes, 0, 0)


def scatter_sum(pieces, axes):
    return jnp.sum(exchange(pieces, axes), 0)


def gather(piece, axes):
    copies = jnp.broadcast_to(piece[None], (lax.axis_size(axes), *piece.shape))
    return exchange(copies, axes)


def gather_sum(piece, axes):
    return jnp.sum(gather(piece, axes), 0)


def shards(activations, out_grads, error, momentum, query):
    rows, cols = error.shape[1:]
    rank = query.shape[1]
    block = rows // BLOCKS
    merged, partial = merge(
        in_hbm(activations.T.reshape(BLOCKS, block, -1)),
        in_hbm(out_grads.T),
        in_hbm(error.reshape(BLOCKS, block, cols)),
        in_hbm(query.T),
    )
    piece = scatter_sum(partial, XC)
    piece = scatter_sum(piece.reshape(8, rank // 8, LANES), Y)
    piece = gather_sum(piece, Z)
    piece = gather(piece, Y).reshape(rank, LANES)
    factor = gather(piece, XC)

    piece = scatter_sum(project(factor, merged), XYC)
    piece, factor = lax.optimization_barrier((piece, factor))
    inverse, weights = invert(factor, lax.axis_size((Z, *XYC)))
    piece = gather_sum(piece, Z)
    piece, weights = lax.optimization_barrier((piece, weights))
    left = spread(factor, weights, block)
    tiles = gather(piece, XYC)
    error_new, momentum_new, query_t = finish(
        inverse, tiles, left, merged, in_hbm(momentum.reshape(BLOCKS, block, cols))
    )
    return (error_new.reshape(error.shape), momentum_new.reshape(momentum.shape), query_t.T)


def solution(mesh):
    fine = Mesh(mesh.devices.reshape(12, 4, 2, 2, 4), ("z", "x", "yl", "c", "yh"))
    rep, shard = ("z", "x", "yl", "c"), "yh"
    return jax.shard_map(
        shards,
        mesh=fine,
        in_specs=(
            P(rep, None),
            P(rep, shard),
            P(rep, None, shard),
            P(None, shard),
            P(shard, None),
        ),
        out_specs=(P(rep, None, shard), P(None, shard), P(shard, None)),
        check_vma=False,
    )
```

```python
import functools
import itertools

import jax
import jax.numpy as jnp
from jax import lax
from jax.experimental import pallas as pl
from jax.experimental.pallas import tpu as pltpu
from jax.sharding import Mesh, PartitionSpec as P

F32, BF16 = jnp.float32, jnp.bfloat16
BLOCKS, GROUP, LANES = 8, 4, 256
XC = ("x", "c")
Y = ("yl", "yh")
XYC = ("x", "yl", "c")
Z = "z"
FIRST = {"z": 9, "x": 2, "yh": 2}
NN = (((1,), (0,)), ((), ()))
NT = (((1,), (1,)), ((), ()))
TN = (((0,), (0,)), ((), ()))


def in_hbm(value):
    return pltpu.with_memory_space_constraint(value, pltpu.HBM)


def params(mib):
    return pltpu.CompilerParams(vmem_limit_bytes=mib << 20)


def cost(flops, size):
    return pl.CostEstimate(flops=flops, bytes_accessed=size, transcendentals=0)


def split(value):
    high = value.astype(BF16)
    return high, (value - high.astype(F32)).astype(BF16)


def dot(left, right, dims):
    return lax.dot_general(left, right, dims, preferred_element_type=F32)


def dot_split(left, right, dims):
    (lh, ll), (rh, rl) = left, right
    return dot(lh, rh, dims) + (dot(lh, rl, dims) + dot(ll, rh, dims))


def dot_full(left, right, dims):
    return lax.dot_general(
        left, right, dims, precision=lax.Precision.HIGHEST, preferred_element_type=F32
    )


def merge_kernel(act_hbm, grad_hbm, err_hbm, query_hbm, merged_ref, partial_ref,
                 act_ref, grad_ref, err_ref, query_ref, sems):
    blocks, rows = merged_ref.shape[:2]
    rank = partial_ref.shape[1]
    small = [
        pltpu.make_async_copy(grad_hbm, grad_ref, sems.at[0]),
        pltpu.make_async_copy(query_hbm, query_ref, sems.at[1]),
    ]
    large = []
    for g in range(0, blocks, GROUP):
        part = pl.ds(g, GROUP)
        large.append([
            pltpu.make_async_copy(act_hbm.at[part], act_ref.at[part], sems.at[2 + g]),
            pltpu.make_async_copy(err_hbm.at[part], err_ref.at[part], sems.at[3 + g]),
        ])
    for copy in [*small, *sum(large, [])]:
        copy.start()
    partial_ref[:, :, rows:] = jnp.zeros((blocks, rank, LANES - rows), F32)
    for copy in small:
        copy.wait()
    stacked = jnp.concatenate(split(query_ref[...]), axis=0)
    for b in range(blocks):
        if b % GROUP == 0:
            for copy in large[b // GROUP]:
                copy.wait()
        merged = dot(act_ref[b], grad_ref[...], NT) + err_ref[b].astype(F32)
        merged_ref[b] = merged
        high, low = split(merged)
        both = dot(stacked, high, NT)
        partial_ref[b, :, :rows] = both[:rank] + (both[rank:] + dot(stacked[:rank], low, NT))


def merge(act, grad, err, query):
    blocks, rows, cols = err.shape
    rank = query.shape[0]
    whole = pl.BlockSpec(memory_space=pltpu.VMEM)
    hbm = pl.BlockSpec(memory_space=pltpu.HBM)
    return pl.pallas_call(
        merge_kernel,
        in_specs=[hbm] * 4,
        out_specs=[whole] * 2,
        out_shape=[
            jax.ShapeDtypeStruct((blocks, rows, cols), F32),
            jax.ShapeDtypeStruct((blocks, rank, LANES), F32),
        ],
        scratch_shapes=[
            *(pltpu.VMEM(value.shape, value.dtype) for value in (act, grad, err, query)),
            pltpu.SemaphoreType.DMA((2 + blocks,)),
        ],
        compiler_params=params(16),
        cost_estimate=cost(500_000_000, 4 << 20),
        name="merge",
    )(act, grad, err, query)


def project_kernel(factor_ref, merged_ref, tiles_ref):
    blocks, rows, cols = merged_ref.shape
    rank = factor_ref.shape[1]
    both, rest = jnp.zeros((2 * rank, cols), F32), jnp.zeros((rank, cols), F32)
    for b in range(blocks):
        stacked = jnp.concatenate(split(factor_ref[b][:, :rows]), axis=0)
        high, low = split(merged_ref[b])
        both += dot(stacked, high, NN)
        rest += dot(stacked[:rank], low, NN)
    total = both[:rank] + (both[rank:] + rest)
    total = jnp.concatenate([total, jnp.zeros((rank, LANES - cols), F32)], axis=1)
    for j in range(tiles_ref.shape[0]):
        r, c = divmod(j, 2)
        tiles_ref[j] = total[8 * r : 8 * r + 8, 128 * c : 128 * c + 128]


def project(factor, merged):
    rank = factor.shape[1]
    whole = pl.BlockSpec(memory_space=pltpu.VMEM)
    return pl.pallas_call(
        project_kernel,
        in_specs=[whole] * 2,
        out_specs=whole,
        out_shape=jax.ShapeDtypeStruct((rank * LANES // 1024, 8, 128), F32),
        compiler_params=params(16),
        cost_estimate=cost(400_000_000, 3 << 20),
        name="project",
    )(factor, merged)


def invert_kernel(replicas, factor_ref, inverse_ref, weights_ref):
    blocks, rank = factor_ref.shape[:2]
    gram = jnp.zeros((rank, rank), F32)
    for b in range(blocks):
        gram += dot_full(factor_ref[b], factor_ref[b], NT)
    lane = lax.broadcasted_iota(jnp.int32, (rank, rank), 1)
    eye = (lane == lax.broadcasted_iota(jnp.int32, (rank, rank), 0)).astype(F32)
    wide = jnp.concatenate([gram, eye], axis=1)
    tiles = [wide[8 * t : 8 * t + 8] for t in range(rank // 8)]
    sub = lax.broadcasted_iota(jnp.int32, (8, 1), 0)
    for k in range(rank):
        at, r = divmod(k, 8)
        row = tiles[at][r : r + 1]
        scaled = row * (1.0 / row[:, k : k + 1])
        for t in range(at, len(tiles)):
            column = tiles[t][:, k : k + 1]
            if t == at:
                column = jnp.where(sub > r, column, 0.0)
            tiles[t] = tiles[t] - column * scaled
    wide = jnp.concatenate(tiles, axis=0)
    pivots = jnp.sum(wide[:, :rank] * eye, axis=1, keepdims=True)
    inverse = wide[:, rank:] / jnp.sqrt(pivots)
    inverse_ref[...] = inverse / replicas
    weights_ref[...] = dot_full(inverse, inverse, TN) / replicas


def invert(factor, replicas):
    rank = factor.shape[1]
    square = jax.ShapeDtypeStruct((rank, rank), F32)
    return pl.pallas_call(
        lambda *refs: invert_kernel(replicas, *refs),
        out_shape=[square, square],
        compiler_params=params(16),
        cost_estimate=cost(7_000_000_000, 1 << 20),
        name="invert",
    )(factor)


def spread_kernel(factor_ref, weights_ref, left_ref):
    blocks, rows = left_ref.shape[:2]
    for b in range(blocks):
        left = split(dot_full(factor_ref[b], weights_ref[...], TN)[:rows])
        left_ref[b] = jnp.concatenate(left, axis=1)


def spread(factor, weights, rows):
    blocks, rank = factor.shape[:2]
    return pl.pallas_call(
        spread_kernel,
        out_shape=jax.ShapeDtypeStruct((blocks, rows, 2 * rank), BF16),
        compiler_params=params(16),
        cost_estimate=cost(2_000_000_000, 1 << 20),
        name="spread",
    )(factor, weights)


def finish_kernel(inverse_ref, tiles_ref, left_ref, merged_ref, mom_hbm,
                  error_hbm, momentum_hbm, query_ref, mom_ref, error_ref, momentum_ref, sems):
    rank, cols = query_ref.shape
    blocks, rows = merged_ref.shape[:2]
    loads, stores = [], []
    for g in range(0, blocks, GROUP):
        part = pl.ds(g, GROUP)
        loads.append(pltpu.make_async_copy(mom_hbm.at[part], mom_ref.at[part], sems.at[0, g // GROUP]))
        stores.append([
            pltpu.make_async_copy(error_ref.at[part], error_hbm.at[part], sems.at[1, g // GROUP]),
            pltpu.make_async_copy(momentum_ref.at[part], momentum_hbm.at[part], sems.at[2, g // GROUP]),
        ])
    for copy in loads:
        copy.start()
    total = jnp.concatenate(
        [
            jnp.concatenate([tiles_ref[j], tiles_ref[j + 1]], axis=1)
            for j in range(0, tiles_ref.shape[0], 2)
        ],
        axis=0,
    )
    high, low = split(total)
    right = jnp.concatenate([high, high, low], axis=0)
    for b in range(blocks):
        left = left_ref[b]
        left = jnp.concatenate([left, left[:, :rank]], axis=1)
        approx = dot(left, right, NN)[:, :cols]
        if b % GROUP == 0:
            loads[b // GROUP].wait()
        error_ref[b] = (merged_ref[b] - approx).astype(BF16)
        momentum_ref[b] = (0.9 * mom_ref[b].astype(F32) + approx).astype(BF16)
        if b % GROUP == GROUP - 1:
            for copy in stores[b // GROUP]:
                copy.start()
    query_ref[...] = dot_full(inverse_ref[...], total, NN)[:, :cols]
    for pair in stores:
        for copy in pair:
            copy.wait()


def finish(inverse, tiles, left, merged, momentum):
    blocks, rows, cols = merged.shape
    rank = inverse.shape[0]
    whole = pl.BlockSpec(memory_space=pltpu.VMEM)
    hbm = pl.BlockSpec(memory_space=pltpu.HBM)
    out = jax.ShapeDtypeStruct((blocks, rows, cols), BF16)
    return pl.pallas_call(
        finish_kernel,
        in_specs=[whole, whole, whole, whole, hbm],
        out_specs=[hbm, hbm, whole],
        out_shape=[out, out, jax.ShapeDtypeStruct((rank, cols), F32)],
        scratch_shapes=[
            *(pltpu.VMEM((blocks, rows, cols), BF16) for _ in range(3)),
            pltpu.SemaphoreType.DMA((3, blocks // GROUP)),
        ],
        compiler_params=params(16),
        cost_estimate=cost(400_000_000, 6 << 20),
        name="finish",
    )(inverse, tiles, left, merged, momentum)


def group_of(axes):
    names = axes if isinstance(axes, tuple) else (axes,)
    sizes = [lax.axis_size(name) for name in names]
    first = [FIRST.get(name, 0) for name in names]
    order = [
        [(f + i) % n for f, i, n in zip(first, index, sizes)]
        for index in itertools.product(*(range(n) for n in sizes))
    ]
    return [[functools.reduce(lambda a, v: a * v[1] + v[0], zip(at, sizes), 0) for at in order]]


def exchange(pieces, axes):
    return lax.all_to_all(pieces, axes, 0, 0, axis_index_groups=group_of(axes))


def scatter_sum(pieces, axes):
    return jnp.sum(exchange(pieces, axes), 0)


def gather(piece, axes):
    copies = jnp.broadcast_to(piece[None], (lax.axis_size(axes), *piece.shape))
    return exchange(copies, axes)


def gather_sum(piece, axes):
    return jnp.sum(gather(piece, axes), 0)


def shards(activations, out_grads, error, momentum, query):
    rows, cols = error.shape[1:]
    rank = query.shape[1]
    block = rows // BLOCKS
    merged, partial = merge(
        in_hbm(activations.T.reshape(BLOCKS, block, -1)),
        in_hbm(out_grads.T),
        in_hbm(error.reshape(BLOCKS, block, cols)),
        in_hbm(query.T),
    )
    piece = scatter_sum(partial, XC)
    piece = scatter_sum(piece.reshape(8, rank // 8, LANES), Y)
    piece = gather_sum(piece, Z)
    piece = gather(piece, Y).reshape(rank, LANES)
    factor = gather(piece, XC)

    piece = scatter_sum(project(factor, merged), XYC)
    piece, factor = lax.optimization_barrier((piece, factor))
    inverse, weights = invert(factor, lax.axis_size((Z, *XYC)))
    piece = gather_sum(piece, Z)
    piece, weights = lax.optimization_barrier((piece, weights))
    left = spread(factor, weights, block)
    tiles = gather(piece, XYC)
    error_new, momentum_new, query_t = finish(
        inverse, tiles, left, merged, in_hbm(momentum.reshape(BLOCKS, block, cols))
    )
    return (error_new.reshape(error.shape), momentum_new.reshape(momentum.shape), query_t.T)


def solution(mesh):
    fine = Mesh(mesh.devices.reshape(12, 4, 2, 2, 4), ("z", "x", "yl", "c", "yh"))
    rep, shard = ("z", "x", "yl", "c"), "yh"
    return jax.shard_map(
        shards,
        mesh=fine,
        in_specs=(
            P(rep, None),
            P(rep, shard),
            P(rep, None, shard),
            P(None, shard),
            P(shard, None),
        ),
        out_specs=(P(rep, None, shard), P(None, shard), P(shard, None)),
        check_vma=False,
    )
```

```python
import functools
import itertools

import jax
import jax.numpy as jnp
from jax import lax
from jax.experimental import pallas as pl
from jax.experimental.pallas import tpu as pltpu
from jax.sharding import Mesh, PartitionSpec as P

F32, BF16 = jnp.float32, jnp.bfloat16
BLOCKS, GROUP, LANES = 8, 4, 256
XC = ("x", "c")
Y = ("yl", "yh")
XYC = ("x", "yl", "c")
Z = "z"
FIRST = {"z": 9, "x": 2, "yh": 2}
NN = (((1,), (0,)), ((), ()))
NT = (((1,), (1,)), ((), ()))
TN = (((0,), (0,)), ((), ()))


def in_hbm(value):
    return pltpu.with_memory_space_constraint(value, pltpu.HBM)


def params(mib):
    return pltpu.CompilerParams(vmem_limit_bytes=mib << 20)


def cost(flops, size):
    return pl.CostEstimate(flops=flops, bytes_accessed=size, transcendentals=0)


def split(value):
    high = value.astype(BF16)
    return high, (value - high.astype(F32)).astype(BF16)


def dot(left, right, dims):
    return lax.dot_general(left, right, dims, preferred_element_type=F32)


def dot_split(left, right, dims):
    (lh, ll), (rh, rl) = left, right
    return dot(lh, rh, dims) + (dot(lh, rl, dims) + dot(ll, rh, dims))


def dot_full(left, right, dims):
    return lax.dot_general(
        left, right, dims, precision=lax.Precision.HIGHEST, preferred_element_type=F32
    )


def merge_kernel(act_hbm, grad_hbm, err_hbm, query_hbm, merged_ref, partial_ref,
                 act_ref, grad_ref, err_ref, query_ref, sems):
    blocks, rows = merged_ref.shape[:2]
    rank = partial_ref.shape[1]
    small = [
        pltpu.make_async_copy(grad_hbm, grad_ref, sems.at[0]),
        pltpu.make_async_copy(query_hbm, query_ref, sems.at[1]),
    ]
    large = []
    for g in range(0, blocks, GROUP):
        part = pl.ds(g, GROUP)
        large.append([
            pltpu.make_async_copy(act_hbm.at[part], act_ref.at[part], sems.at[2 + g]),
            pltpu.make_async_copy(err_hbm.at[part], err_ref.at[part], sems.at[3 + g]),
        ])
    for copy in [*small, *sum(large, [])]:
        copy.start()
    partial_ref[:, :, rows:] = jnp.zeros((blocks, rank, LANES - rows), F32)
    for copy in small:
        copy.wait()
    stacked = jnp.concatenate(split(query_ref[...]), axis=0)
    grad_t = grad_ref[...].astype(F32).T.astype(BF16)
    for b in range(blocks):
        if b % GROUP == 0:
            for copy in large[b // GROUP]:
                copy.wait()
        merged = dot(act_ref[b], grad_t, NN) + err_ref[b].astype(F32)
        merged_ref[b] = merged
        high, low = split(merged)
        both = dot(stacked, high, NT)
        partial_ref[b, :, :rows] = both[:rank] + (both[rank:] + dot(stacked[:rank], low, NT))


def merge(act, grad, err, query):
    blocks, rows, cols = err.shape
    rank = query.shape[0]
    whole = pl.BlockSpec(memory_space=pltpu.VMEM)
    hbm = pl.BlockSpec(memory_space=pltpu.HBM)
    return pl.pallas_call(
        merge_kernel,
        in_specs=[hbm] * 4,
        out_specs=[whole] * 2,
        out_shape=[
            jax.ShapeDtypeStruct((blocks, rows, cols), F32),
            jax.ShapeDtypeStruct((blocks, rank, LANES), F32),
        ],
        scratch_shapes=[
            *(pltpu.VMEM(value.shape, value.dtype) for value in (act, grad, err, query)),
            pltpu.SemaphoreType.DMA((2 + blocks,)),
        ],
        compiler_params=params(16),
        cost_estimate=cost(500_000_000, 4 << 20),
        name="merge",
    )(act, grad, err, query)


def project_kernel(factor_ref, merged_ref, tiles_ref):
    blocks, rows, cols = merged_ref.shape
    rank = factor_ref.shape[1]
    both, rest = jnp.zeros((2 * rank, cols), F32), jnp.zeros((rank, cols), F32)
    for b in range(blocks):
        stacked = jnp.concatenate(split(factor_ref[b][:, :rows]), axis=0)
        high, low = split(merged_ref[b])
        both += dot(stacked, high, NN)
        rest += dot(stacked[:rank], low, NN)
    total = both[:rank] + (both[rank:] + rest)
    total = jnp.concatenate([total, jnp.zeros((rank, LANES - cols), F32)], axis=1)
    for j in range(tiles_ref.shape[0]):
        r, c = divmod(j, 2)
        tiles_ref[j] = total[8 * r : 8 * r + 8, 128 * c : 128 * c + 128]


def project(factor, merged):
    rank = factor.shape[1]
    whole = pl.BlockSpec(memory_space=pltpu.VMEM)
    return pl.pallas_call(
        project_kernel,
        in_specs=[whole] * 2,
        out_specs=whole,
        out_shape=jax.ShapeDtypeStruct((rank * LANES // 1024, 8, 128), F32),
        compiler_params=params(16),
        cost_estimate=cost(400_000_000, 3 << 20),
        name="project",
    )(factor, merged)


def invert_kernel(replicas, factor_ref, inverse_ref, weights_ref):
    blocks, rank = factor_ref.shape[:2]
    gram = jnp.zeros((rank, rank), F32)
    for b in range(blocks):
        gram += dot_full(factor_ref[b], factor_ref[b], NT)
    lane = lax.broadcasted_iota(jnp.int32, (rank, rank), 1)
    eye = (lane == lax.broadcasted_iota(jnp.int32, (rank, rank), 0)).astype(F32)
    wide = jnp.concatenate([gram, eye], axis=1)
    tiles = [wide[8 * t : 8 * t + 8] for t in range(rank // 8)]
    sub = lax.broadcasted_iota(jnp.int32, (8, 1), 0)
    for k in range(rank):
        at, r = divmod(k, 8)
        row = tiles[at][r : r + 1]
        scaled = row * (1.0 / row[:, k : k + 1])
        for t in range(at, len(tiles)):
            column = tiles[t][:, k : k + 1]
            if t == at:
                column = jnp.where(sub > r, column, 0.0)
            tiles[t] = tiles[t] - column * scaled
    wide = jnp.concatenate(tiles, axis=0)
    pivots = jnp.sum(wide[:, :rank] * eye, axis=1, keepdims=True)
    inverse = wide[:, rank:] / jnp.sqrt(pivots)
    inverse_ref[...] = inverse / replicas
    weights_ref[...] = dot_full(inverse, inverse, TN) / replicas


def invert(factor, replicas):
    rank = factor.shape[1]
    square = jax.ShapeDtypeStruct((rank, rank), F32)
    return pl.pallas_call(
        lambda *refs: invert_kernel(replicas, *refs),
        out_shape=[square, square],
        compiler_params=params(16),
        cost_estimate=cost(7_000_000_000, 1 << 20),
        name="invert",
    )(factor)


def spread_kernel(factor_ref, weights_ref, left_ref):
    blocks, rows = left_ref.shape[:2]
    for b in range(blocks):
        left = split(dot_full(factor_ref[b], weights_ref[...], TN)[:rows])
        left_ref[b] = jnp.concatenate(left, axis=1)


def spread(factor, weights, rows):
    blocks, rank = factor.shape[:2]
    return pl.pallas_call(
        spread_kernel,
        out_shape=jax.ShapeDtypeStruct((blocks, rows, 2 * rank), BF16),
        compiler_params=params(16),
        cost_estimate=cost(2_000_000_000, 1 << 20),
        name="spread",
    )(factor, weights)


def finish_kernel(inverse_ref, tiles_ref, left_ref, merged_ref, mom_hbm,
                  error_hbm, momentum_hbm, query_ref, mom_ref, error_ref, momentum_ref, sems):
    rank, cols = query_ref.shape
    blocks, rows = merged_ref.shape[:2]
    loads, stores = [], []
    for g in range(0, blocks, GROUP):
        part = pl.ds(g, GROUP)
        loads.append(pltpu.make_async_copy(mom_hbm.at[part], mom_ref.at[part], sems.at[0, g // GROUP]))
        stores.append([
            pltpu.make_async_copy(error_ref.at[part], error_hbm.at[part], sems.at[1, g // GROUP]),
            pltpu.make_async_copy(momentum_ref.at[part], momentum_hbm.at[part], sems.at[2, g // GROUP]),
        ])
    for copy in loads:
        copy.start()
    total = jnp.concatenate(
        [
            jnp.concatenate([tiles_ref[j], tiles_ref[j + 1]], axis=1)
            for j in range(0, tiles_ref.shape[0], 2)
        ],
        axis=0,
    )
    high, low = split(total)
    right = jnp.concatenate([high, high, low], axis=0)
    for b in range(blocks):
        left = left_ref[b]
        left = jnp.concatenate([left, left[:, :rank]], axis=1)
        approx = dot(left, right, NN)[:, :cols]
        if b % GROUP == 0:
            loads[b // GROUP].wait()
        error_ref[b] = (merged_ref[b] - approx).astype(BF16)
        momentum_ref[b] = (0.9 * mom_ref[b].astype(F32) + approx).astype(BF16)
        if b % GROUP == GROUP - 1:
            for copy in stores[b // GROUP]:
                copy.start()
    query_ref[...] = dot_full(inverse_ref[...], total, NN)[:, :cols]
    for pair in stores:
        for copy in pair:
            copy.wait()


def finish(inverse, tiles, left, merged, momentum):
    blocks, rows, cols = merged.shape
    rank = inverse.shape[0]
    whole = pl.BlockSpec(memory_space=pltpu.VMEM)
    hbm = pl.BlockSpec(memory_space=pltpu.HBM)
    out = jax.ShapeDtypeStruct((blocks, rows, cols), BF16)
    return pl.pallas_call(
        finish_kernel,
        in_specs=[whole, whole, whole, whole, hbm],
        out_specs=[hbm, hbm, whole],
        out_shape=[out, out, jax.ShapeDtypeStruct((rank, cols), F32)],
        scratch_shapes=[
            *(pltpu.VMEM((blocks, rows, cols), BF16) for _ in range(3)),
            pltpu.SemaphoreType.DMA((3, blocks // GROUP)),
        ],
        compiler_params=params(16),
        cost_estimate=cost(400_000_000, 6 << 20),
        name="finish",
    )(inverse, tiles, left, merged, momentum)


def group_of(axes):
    names = axes if isinstance(axes, tuple) else (axes,)
    sizes = [lax.axis_size(name) for name in names]
    first = [FIRST.get(name, 0) for name in names]
    order = [
        [(f + i) % n for f, i, n in zip(first, reversed(index), sizes)]
        for index in itertools.product(*(range(n) for n in reversed(sizes)))
    ]
    return [[functools.reduce(lambda a, v: a * v[1] + v[0], zip(at, sizes), 0) for at in order]]


def exchange(pieces, axes):
    return lax.all_to_all(pieces, axes, 0, 0, axis_index_groups=group_of(axes))


def scatter_sum(pieces, axes):
    return jnp.sum(exchange(pieces, axes), 0)


def gather(piece, axes):
    copies = jnp.broadcast_to(piece[None], (lax.axis_size(axes), *piece.shape))
    return exchange(copies, axes)


def gather_sum(piece, axes):
    return jnp.sum(gather(piece, axes), 0)


def shards(activations, out_grads, error, momentum, query):
    rows, cols = error.shape[1:]
    rank = query.shape[1]
    block = rows // BLOCKS
    merged, partial = merge(
        in_hbm(activations.T.reshape(BLOCKS, block, -1)),
        in_hbm(out_grads.T),
        in_hbm(error.reshape(BLOCKS, block, cols)),
        in_hbm(query.T),
    )
    piece = scatter_sum(partial, XC)
    piece = scatter_sum(piece.reshape(8, rank // 8, LANES), Y)
    piece = gather_sum(piece, Z)
    piece = gather(piece, Y).reshape(rank, LANES)
    factor = lax.all_gather(gather(piece, "x"), "c", tiled=True)

    piece = scatter_sum(project(factor, merged), XYC)
    piece, factor = lax.optimization_barrier((piece, factor))
    inverse, weights = invert(factor, lax.axis_size((Z, *XYC)))
    piece = gather_sum(piece, Z)
    piece, weights = lax.optimization_barrier((piece, weights))
    left = spread(factor, weights, block)
    tiles = gather(piece, XYC)
    error_new, momentum_new, query_t = finish(
        inverse, tiles, left, merged, in_hbm(momentum.reshape(BLOCKS, block, cols))
    )
    return (error_new.reshape(error.shape), momentum_new.reshape(momentum.shape), query_t.T)


def solution(mesh):
    fine = Mesh(mesh.devices.reshape(12, 4, 2, 2, 4), ("z", "x", "yl", "c", "yh"))
    rep, shard = ("z", "x", "yl", "c"), "yh"
    return jax.shard_map(
        shards,
        mesh=fine,
        in_specs=(
            P(rep, None),
            P(rep, shard),
            P(rep, None, shard),
            P(None, shard),
            P(shard, None),
        ),
        out_specs=(P(rep, None, shard), P(None, shard), P(shard, None)),
        check_vma=False,
    )
```

```python
import functools
import itertools

import jax
import jax.numpy as jnp
from jax import lax
from jax.experimental import pallas as pl
from jax.experimental.pallas import tpu as pltpu
from jax.sharding import Mesh, PartitionSpec as P

F32, BF16 = jnp.float32, jnp.bfloat16
BLOCKS, GROUP, PART, LANES = 8, 4, 2, 256
Y = ("yl", "yh")
XYC = ("x", "yl", "c")
Z = "z"
FIRST = {"z": 9, "x": 2, "yh": 2}
NN = (((1,), (0,)), ((), ()))
NT = (((1,), (1,)), ((), ()))
TN = (((0,), (0,)), ((), ()))


def in_hbm(value):
    return pltpu.with_memory_space_constraint(value, pltpu.HBM)


def params(mib):
    return pltpu.CompilerParams(vmem_limit_bytes=mib << 20)


def cost(flops, size):
    return pl.CostEstimate(flops=flops, bytes_accessed=size, transcendentals=0)


def split(value):
    high = value.astype(BF16)
    return high, (value - high.astype(F32)).astype(BF16)


def dot(left, right, dims):
    return lax.dot_general(left, right, dims, preferred_element_type=F32)


def dot_split(left, right, dims):
    (lh, ll), (rh, rl) = left, right
    return dot(lh, rh, dims) + (dot(lh, rl, dims) + dot(ll, rh, dims))


def dot_full(left, right, dims):
    return lax.dot_general(
        left, right, dims, precision=lax.Precision.HIGHEST, preferred_element_type=F32
    )


def half_start(other):
    core = lax.axis_index("c")
    return GROUP * (1 - core if other else core)


def merge_kernel(other, act_hbm, grad_hbm, err_hbm, query_hbm, merged_ref, partial_ref,
                 act_ref, grad_ref, err_ref, query_ref, sems):
    rows = merged_ref.shape[1]
    rank = partial_ref.shape[1]
    start = half_start(other)
    small = [
        pltpu.make_async_copy(grad_hbm, grad_ref, sems.at[0]),
        pltpu.make_async_copy(query_hbm, query_ref, sems.at[1]),
    ]
    large = []
    for g in range(0, GROUP, PART):
        source, target = pl.ds(start + g, PART), pl.ds(g, PART)
        large.append([
            pltpu.make_async_copy(act_hbm.at[source], act_ref.at[target], sems.at[2 + g]),
            pltpu.make_async_copy(err_hbm.at[source], err_ref.at[target], sems.at[3 + g]),
        ])
    for copy in [*small, *sum(large, [])]:
        copy.start()
    partial_ref[:, :, rows:] = jnp.zeros((GROUP, rank, LANES - rows), F32)
    for copy in small:
        copy.wait()
    stacked = jnp.concatenate(split(query_ref[...]), axis=0)
    grad_t = grad_ref[...].astype(F32).T.astype(BF16)
    for b in range(GROUP):
        if b % PART == 0:
            for copy in large[b // PART]:
                copy.wait()
        merged = dot(act_ref[b], grad_t, NN) + err_ref[b].astype(F32)
        merged_ref[b] = merged
        high, low = split(merged)
        both = dot(stacked, high, NT)
        partial_ref[b, :, :rows] = both[:rank] + (both[rank:] + dot(stacked[:rank], low, NT))


def merge(act, grad, err, query, other):
    rows, cols = err.shape[1:]
    tok, rank = act.shape[2], query.shape[0]
    whole = pl.BlockSpec(memory_space=pltpu.VMEM)
    hbm = pl.BlockSpec(memory_space=pltpu.HBM)
    return pl.pallas_call(
        functools.partial(merge_kernel, other),
        in_specs=[hbm] * 4,
        out_specs=[whole] * 2,
        out_shape=[
            jax.ShapeDtypeStruct((GROUP, rows, cols), F32),
            jax.ShapeDtypeStruct((GROUP, rank, LANES), F32),
        ],
        scratch_shapes=[
            pltpu.VMEM((GROUP, rows, tok), BF16),
            pltpu.VMEM(grad.shape, BF16),
            pltpu.VMEM((GROUP, rows, cols), BF16),
            pltpu.VMEM(query.shape, F32),
            pltpu.SemaphoreType.DMA((2 + GROUP,)),
        ],
        compiler_params=params(16),
        cost_estimate=cost(300_000_000, 3 << 20),
        name="merge_other" if other else "merge_own",
    )(act, grad, err, query)


def project_kernel(factor_ref, own_ref, other_ref, tiles_ref):
    rows, cols = own_ref.shape[1:]
    rank = factor_ref.shape[1]
    both, rest = jnp.zeros((2 * rank, cols), F32), jnp.zeros((rank, cols), F32)
    for b in range(2 * GROUP):
        merged_ref = other_ref if b >= GROUP else own_ref
        factor = factor_ref[half_start(b >= GROUP) + b % GROUP]
        stacked = jnp.concatenate(split(factor[:, :rows]), axis=0)
        high, low = split(merged_ref[b % GROUP])
        both += dot(stacked, high, NN)
        rest += dot(stacked[:rank], low, NN)
    total = both[:rank] + (both[rank:] + rest)
    total = jnp.concatenate([total, jnp.zeros((rank, LANES - cols), F32)], axis=1)
    for j in range(tiles_ref.shape[0]):
        r, c = divmod(j, 2)
        tiles_ref[j] = total[8 * r : 8 * r + 8, 128 * c : 128 * c + 128]


def project(factor, own, other):
    rank = factor.shape[1]
    whole = pl.BlockSpec(memory_space=pltpu.VMEM)
    return pl.pallas_call(
        project_kernel,
        in_specs=[whole] * 3,
        out_specs=whole,
        out_shape=jax.ShapeDtypeStruct((rank * LANES // 1024, 8, 128), F32),
        compiler_params=params(16),
        cost_estimate=cost(400_000_000, 3 << 20),
        name="project",
    )(factor, own, other)


def invert_kernel(replicas, factor_ref, inverse_ref, weights_ref):
    blocks, rank = factor_ref.shape[:2]
    gram = jnp.zeros((rank, rank), F32)
    for b in range(blocks):
        gram += dot_full(factor_ref[b], factor_ref[b], NT)
    lane = lax.broadcasted_iota(jnp.int32, (rank, rank), 1)
    eye = (lane == lax.broadcasted_iota(jnp.int32, (rank, rank), 0)).astype(F32)
    wide = jnp.concatenate([gram, eye], axis=1)
    tiles = [wide[8 * t : 8 * t + 8] for t in range(rank // 8)]
    sub = lax.broadcasted_iota(jnp.int32, (8, 1), 0)
    for k in range(rank):
        at, r = divmod(k, 8)
        row = tiles[at][r : r + 1]
        scaled = row * (1.0 / row[:, k : k + 1])
        for t in range(at, len(tiles)):
            column = tiles[t][:, k : k + 1]
            if t == at:
                column = jnp.where(sub > r, column, 0.0)
            tiles[t] = tiles[t] - column * scaled
    wide = jnp.concatenate(tiles, axis=0)
    pivots = jnp.sum(wide[:, :rank] * eye, axis=1, keepdims=True)
    inverse = wide[:, rank:] / jnp.sqrt(pivots)
    inverse_ref[...] = inverse / replicas
    weights_ref[...] = dot_full(inverse, inverse, TN) / replicas


def invert(factor, replicas):
    rank = factor.shape[1]
    square = jax.ShapeDtypeStruct((rank, rank), F32)
    return pl.pallas_call(
        lambda *refs: invert_kernel(replicas, *refs),
        out_shape=[square, square],
        compiler_params=params(16),
        cost_estimate=cost(7_000_000_000, 1 << 20),
        name="invert",
    )(factor)


def spread_kernel(factor_ref, weights_ref, left_ref):
    blocks, rows = left_ref.shape[:2]
    for b in range(blocks):
        left = split(dot_full(factor_ref[b], weights_ref[...], TN)[:rows])
        left_ref[b] = jnp.concatenate(left, axis=1)


def spread(factor, weights, rows):
    blocks, rank = factor.shape[:2]
    return pl.pallas_call(
        spread_kernel,
        out_shape=jax.ShapeDtypeStruct((blocks, rows, 2 * rank), BF16),
        compiler_params=params(16),
        cost_estimate=cost(2_000_000_000, 1 << 20),
        name="spread",
    )(factor, weights)


def finish_kernel(inverse_ref, tiles_ref, left_ref, own_ref, other_ref, mom_hbm,
                  error_hbm, momentum_hbm, query_ref, mom_ref, error_ref, momentum_ref, sems):
    rank, cols = query_ref.shape
    loads, stores = [], []
    for half in range(2):
        far, near = pl.ds(half_start(half), GROUP), pl.ds(half * GROUP, GROUP)
        loads.append(pltpu.make_async_copy(mom_hbm.at[far], mom_ref.at[near], sems.at[0, half]))
        stores.append([
            pltpu.make_async_copy(error_ref.at[near], error_hbm.at[far], sems.at[1, half]),
            pltpu.make_async_copy(momentum_ref.at[near], momentum_hbm.at[far], sems.at[2, half]),
        ])
    for copy in loads:
        copy.start()
    total = jnp.concatenate(
        [
            jnp.concatenate([tiles_ref[j], tiles_ref[j + 1]], axis=1)
            for j in range(0, tiles_ref.shape[0], 2)
        ],
        axis=0,
    )
    high, low = split(total)
    right = jnp.concatenate([high, high, low], axis=0)
    for b in range(2 * GROUP):
        half, at = divmod(b, GROUP)
        merged_ref = other_ref if half else own_ref
        left = left_ref[half_start(half) + at]
        left = jnp.concatenate([left, left[:, :rank]], axis=1)
        approx = dot(left, right, NN)[:, :cols]
        if at == 0:
            loads[half].wait()
        error_ref[b] = (merged_ref[at] - approx).astype(BF16)
        momentum_ref[b] = (0.9 * mom_ref[b].astype(F32) + approx).astype(BF16)
        if at == GROUP - 1:
            for copy in stores[half]:
                copy.start()
    query_ref[...] = dot_full(inverse_ref[...], total, NN)[:, :cols]
    for pair in stores:
        for copy in pair:
            copy.wait()


def finish(inverse, tiles, left, own, other, momentum):
    blocks, rows, cols = momentum.shape
    rank = inverse.shape[0]
    whole = pl.BlockSpec(memory_space=pltpu.VMEM)
    hbm = pl.BlockSpec(memory_space=pltpu.HBM)
    out = jax.ShapeDtypeStruct((blocks, rows, cols), BF16)
    return pl.pallas_call(
        finish_kernel,
        in_specs=[whole] * 5 + [hbm],
        out_specs=[hbm, hbm, whole],
        out_shape=[out, out, jax.ShapeDtypeStruct((rank, cols), F32)],
        scratch_shapes=[
            *(pltpu.VMEM((blocks, rows, cols), BF16) for _ in range(3)),
            pltpu.SemaphoreType.DMA((3, 2)),
        ],
        compiler_params=params(16),
        cost_estimate=cost(400_000_000, 6 << 20),
        name="finish",
    )(inverse, tiles, left, own, other, momentum)


def group_of(axes):
    names = axes if isinstance(axes, tuple) else (axes,)
    sizes = [lax.axis_size(name) for name in names]
    first = [FIRST.get(name, 0) for name in names]
    order = [
        [(f + i) % n for f, i, n in zip(first, index, sizes)]
        for index in itertools.product(*(range(n) for n in sizes))
    ]
    return [[functools.reduce(lambda a, v: a * v[1] + v[0], zip(at, sizes), 0) for at in order]]


def exchange(pieces, axes):
    return lax.all_to_all(pieces, axes, 0, 0, axis_index_groups=group_of(axes))


def scatter_sum(pieces, axes):
    return jnp.sum(exchange(pieces, axes), 0)


def gather(piece, axes):
    copies = jnp.broadcast_to(piece[None], (lax.axis_size(axes), *piece.shape))
    return exchange(copies, axes)


def gather_sum(piece, axes):
    return jnp.sum(gather(piece, axes), 0)


def shards(activations, out_grads, error, momentum, query):
    rows, cols = error.shape[1:]
    rank = query.shape[1]
    block = rows // BLOCKS
    inputs = (
        in_hbm(activations.T.reshape(BLOCKS, block, -1)),
        in_hbm(out_grads.T),
        in_hbm(error.reshape(BLOCKS, block, cols)),
        in_hbm(query.T),
    )
    other, partial = merge(*inputs, True)
    arrived = lax.ppermute(partial, "c", [(0, 1), (1, 0)])
    own, partial = merge(*inputs, False)
    piece = scatter_sum(partial + arrived, "x")
    piece = scatter_sum(piece.reshape(8, rank // 8, LANES), Y)
    piece = gather_sum(piece, Z)
    piece = gather(piece, Y).reshape(rank, LANES)
    factor = lax.all_gather(gather(piece, "x"), "c", tiled=True)

    piece = scatter_sum(project(factor, own, other), XYC)
    piece, factor = lax.optimization_barrier((piece, factor))
    inverse, weights = invert(factor, lax.axis_size((Z, *XYC)))
    piece = gather_sum(piece, Z)
    piece, weights = lax.optimization_barrier((piece, weights))
    left = spread(factor, weights, block)
    tiles = gather(piece, XYC)
    error_new, momentum_new, query_t = finish(
        inverse, tiles, left, own, other, in_hbm(momentum.reshape(BLOCKS, block, cols))
    )
    return (error_new.reshape(error.shape), momentum_new.reshape(momentum.shape), query_t.T)


def solution(mesh):
    fine = Mesh(mesh.devices.reshape(12, 4, 2, 2, 4), ("z", "x", "yl", "c", "yh"))
    rep, shard = ("z", "x", "yl", "c"), "yh"
    return jax.shard_map(
        shards,
        mesh=fine,
        in_specs=(
            P(rep, None),
            P(rep, shard),
            P(rep, None, shard),
            P(None, shard),
            P(shard, None),
        ),
        out_specs=(P(rep, None, shard), P(None, shard), P(shard, None)),
        check_vma=False,
    )
```

```python
import functools
import itertools

import jax
import jax.numpy as jnp
from jax import lax
from jax.experimental import pallas as pl
from jax.experimental.pallas import tpu as pltpu
from jax.sharding import Mesh, PartitionSpec as P

F32, BF16 = jnp.float32, jnp.bfloat16
BLOCKS, GROUP, LANES = 8, 4, 256
XC = ("x", "c")
Y = ("yl", "yh")
XYC = ("x", "yl", "c")
Z = "z"
FIRST = {"z": 9, "x": 2, "yh": 2}
NN = (((1,), (0,)), ((), ()))
NT = (((1,), (1,)), ((), ()))
TN = (((0,), (0,)), ((), ()))


def in_hbm(value):
    return pltpu.with_memory_space_constraint(value, pltpu.HBM)


def params(mib):
    return pltpu.CompilerParams(vmem_limit_bytes=mib << 20)


def cost(flops, size):
    return pl.CostEstimate(flops=flops, bytes_accessed=size, transcendentals=0)


def split(value):
    high = value.astype(BF16)
    return high, (value - high.astype(F32)).astype(BF16)


def dot(left, right, dims):
    return lax.dot_general(left, right, dims, preferred_element_type=F32)


def dot_split(left, right, dims):
    (lh, ll), (rh, rl) = left, right
    return dot(lh, rh, dims) + (dot(lh, rl, dims) + dot(ll, rh, dims))


def dot_full(left, right, dims):
    return lax.dot_general(
        left, right, dims, precision=lax.Precision.HIGHEST, preferred_element_type=F32
    )


def merge_kernel(act_hbm, grad_hbm, err_hbm, query_hbm, merged_ref, partial_ref,
                 act_ref, grad_ref, err_ref, query_ref, sems):
    blocks, rows = merged_ref.shape[:2]
    rank = partial_ref.shape[1]
    small = [
        pltpu.make_async_copy(grad_hbm, grad_ref, sems.at[0]),
        pltpu.make_async_copy(query_hbm, query_ref, sems.at[1]),
    ]
    large = []
    for g in range(0, blocks, GROUP):
        part = pl.ds(g, GROUP)
        large.append([
            pltpu.make_async_copy(act_hbm.at[part], act_ref.at[part], sems.at[2 + g]),
            pltpu.make_async_copy(err_hbm.at[part], err_ref.at[part], sems.at[3 + g]),
        ])
    for copy in [*small, *sum(large, [])]:
        copy.start()
    partial_ref[:, :, rows:] = jnp.zeros((blocks, rank, LANES - rows), F32)
    for copy in small:
        copy.wait()
    stacked = jnp.concatenate(split(query_ref[...]), axis=0)
    grad_t = grad_ref[...].astype(F32).T.astype(BF16)
    for b in range(blocks):
        if b % GROUP == 0:
            for copy in large[b // GROUP]:
                copy.wait()
        merged = dot(act_ref[b], grad_t, NN) + err_ref[b].astype(F32)
        merged_ref[b] = merged
        high, low = split(merged)
        both = dot(stacked, high, NT)
        partial_ref[b, :, :rows] = both[:rank] + (both[rank:] + dot(stacked[:rank], low, NT))


def merge(act, grad, err, query):
    blocks, rows, cols = err.shape
    rank = query.shape[0]
    whole = pl.BlockSpec(memory_space=pltpu.VMEM)
    hbm = pl.BlockSpec(memory_space=pltpu.HBM)
    return pl.pallas_call(
        merge_kernel,
        in_specs=[hbm] * 4,
        out_specs=[whole] * 2,
        out_shape=[
            jax.ShapeDtypeStruct((blocks, rows, cols), F32),
            jax.ShapeDtypeStruct((blocks, rank, LANES), F32),
        ],
        scratch_shapes=[
            *(pltpu.VMEM(value.shape, value.dtype) for value in (act, grad, err, query)),
            pltpu.SemaphoreType.DMA((2 + blocks,)),
        ],
        compiler_params=params(16),
        cost_estimate=cost(500_000_000, 4 << 20),
        name="merge",
    )(act, grad, err, query)


def project_kernel(factor_ref, merged_ref, tiles_ref):
    blocks, rows, cols = merged_ref.shape
    rank = factor_ref.shape[1]
    both, rest = jnp.zeros((2 * rank, cols), F32), jnp.zeros((rank, cols), F32)
    for b in range(blocks):
        stacked = jnp.concatenate(split(factor_ref[b][:, :rows]), axis=0)
        high, low = split(merged_ref[b])
        both += dot(stacked, high, NN)
        rest += dot(stacked[:rank], low, NN)
    total = both[:rank] + (both[rank:] + rest)
    total = jnp.concatenate([total, jnp.zeros((rank, LANES - cols), F32)], axis=1)
    for j in range(tiles_ref.shape[0]):
        r, c = divmod(j, 2)
        tiles_ref[j] = total[8 * r : 8 * r + 8, 128 * c : 128 * c + 128]


def project(factor, merged):
    rank = factor.shape[1]
    whole = pl.BlockSpec(memory_space=pltpu.VMEM)
    return pl.pallas_call(
        project_kernel,
        in_specs=[whole] * 2,
        out_specs=whole,
        out_shape=jax.ShapeDtypeStruct((rank * LANES // 1024, 8, 128), F32),
        compiler_params=params(16),
        cost_estimate=cost(400_000_000, 3 << 20),
        name="project",
    )(factor, merged)


def invert_kernel(replicas, factor_ref, inverse_ref, weights_ref):
    blocks, rank = factor_ref.shape[:2]
    gram = jnp.zeros((rank, rank), F32)
    for b in range(blocks):
        gram += dot_full(factor_ref[b], factor_ref[b], NT)
    lane = lax.broadcasted_iota(jnp.int32, (rank, rank), 1)
    eye = (lane == lax.broadcasted_iota(jnp.int32, (rank, rank), 0)).astype(F32)
    wide = jnp.concatenate([gram, eye], axis=1)
    tiles = [wide[8 * t : 8 * t + 8] for t in range(rank // 8)]
    sub = lax.broadcasted_iota(jnp.int32, (8, 1), 0)
    for k in range(rank):
        at, r = divmod(k, 8)
        row = tiles[at][r : r + 1]
        scaled = row * (1.0 / row[:, k : k + 1])
        for t in range(at, len(tiles)):
            column = tiles[t][:, k : k + 1]
            if t == at:
                column = jnp.where(sub > r, column, 0.0)
            tiles[t] = tiles[t] - column * scaled
    wide = jnp.concatenate(tiles, axis=0)
    pivots = jnp.sum(wide[:, :rank] * eye, axis=1, keepdims=True)
    inverse = wide[:, rank:] / jnp.sqrt(pivots)
    inverse_ref[...] = inverse / replicas
    weights_ref[...] = dot_full(inverse, inverse, TN) / replicas


def invert(factor, replicas):
    rank = factor.shape[1]
    square = jax.ShapeDtypeStruct((rank, rank), F32)
    return pl.pallas_call(
        lambda *refs: invert_kernel(replicas, *refs),
        out_shape=[square, square],
        compiler_params=params(16),
        cost_estimate=cost(7_000_000_000, 1 << 20),
        name="invert",
    )(factor)


def spread_kernel(factor_ref, weights_ref, left_ref):
    blocks, rows = left_ref.shape[:2]
    for b in range(blocks):
        left = split(dot_full(factor_ref[b], weights_ref[...], TN)[:rows])
        left_ref[b] = jnp.concatenate(left, axis=1)


def spread(factor, weights, rows):
    blocks, rank = factor.shape[:2]
    return pl.pallas_call(
        spread_kernel,
        out_shape=jax.ShapeDtypeStruct((blocks, rows, 2 * rank), BF16),
        compiler_params=params(16),
        cost_estimate=cost(2_000_000_000, 1 << 20),
        name="spread",
    )(factor, weights)


def finish_kernel(inverse_ref, tiles_ref, left_ref, merged_ref, mom_hbm,
                  error_hbm, momentum_hbm, query_ref, mom_ref, error_ref, momentum_ref, sems):
    rank, cols = query_ref.shape
    blocks, rows = merged_ref.shape[:2]
    loads, stores = [], []
    for g in range(0, blocks, GROUP):
        part = pl.ds(g, GROUP)
        loads.append(pltpu.make_async_copy(mom_hbm.at[part], mom_ref.at[part], sems.at[0, g // GROUP]))
        stores.append([
            pltpu.make_async_copy(error_ref.at[part], error_hbm.at[part], sems.at[1, g // GROUP]),
            pltpu.make_async_copy(momentum_ref.at[part], momentum_hbm.at[part], sems.at[2, g // GROUP]),
        ])
    for copy in loads:
        copy.start()
    total = jnp.concatenate(
        [
            jnp.concatenate([tiles_ref[j], tiles_ref[j + 1]], axis=1)
            for j in range(0, tiles_ref.shape[0], 2)
        ],
        axis=0,
    )
    high, low = split(total)
    right = jnp.concatenate([high, high, low], axis=0)
    for b in range(blocks):
        left = left_ref[b]
        left = jnp.concatenate([left, left[:, :rank]], axis=1)
        approx = dot(left, right, NN)[:, :cols]
        if b % GROUP == 0:
            loads[b // GROUP].wait()
        error_ref[b] = (merged_ref[b] - approx).astype(BF16)
        momentum_ref[b] = (0.9 * mom_ref[b].astype(F32) + approx).astype(BF16)
        if b % GROUP == GROUP - 1:
            for copy in stores[b // GROUP]:
                copy.start()
    query_ref[...] = dot_full(inverse_ref[...], total, NN)[:, :cols]
    for pair in stores:
        for copy in pair:
            copy.wait()


def finish(inverse, tiles, left, merged, momentum):
    blocks, rows, cols = merged.shape
    rank = inverse.shape[0]
    whole = pl.BlockSpec(memory_space=pltpu.VMEM)
    hbm = pl.BlockSpec(memory_space=pltpu.HBM)
    out = jax.ShapeDtypeStruct((blocks, rows, cols), BF16)
    return pl.pallas_call(
        finish_kernel,
        in_specs=[whole, whole, whole, whole, hbm],
        out_specs=[hbm, hbm, whole],
        out_shape=[out, out, jax.ShapeDtypeStruct((rank, cols), F32)],
        scratch_shapes=[
            *(pltpu.VMEM((blocks, rows, cols), BF16) for _ in range(3)),
            pltpu.SemaphoreType.DMA((3, blocks // GROUP)),
        ],
        compiler_params=params(16),
        cost_estimate=cost(400_000_000, 6 << 20),
        name="finish",
    )(inverse, tiles, left, merged, momentum)


def group_of(axes):
    names = axes if isinstance(axes, tuple) else (axes,)
    sizes = [lax.axis_size(name) for name in names]
    first = [FIRST.get(name, 0) for name in names]
    order = [
        [(f + i) % n for f, i, n in zip(first, index, sizes)]
        for index in itertools.product(*(range(n) for n in sizes))
    ]
    if names == XC:
        order.sort(key=lambda at: at[1])
    return [[functools.reduce(lambda a, v: a * v[1] + v[0], zip(at, sizes), 0) for at in order]]


def exchange(pieces, axes):
    return lax.all_to_all(pieces, axes, 0, 0, axis_index_groups=group_of(axes))


def scatter_sum(pieces, axes):
    return jnp.sum(exchange(pieces, axes), 0)


def gather(piece, axes):
    copies = jnp.broadcast_to(piece[None], (lax.axis_size(axes), *piece.shape))
    return exchange(copies, axes)


def gather_sum(piece, axes):
    return jnp.sum(gather(piece, axes), 0)


def shards(activations, out_grads, error, momentum, query):
    rows, cols = error.shape[1:]
    rank = query.shape[1]
    block = rows // BLOCKS
    merged, partial = merge(
        in_hbm(activations.T.reshape(BLOCKS, block, -1)),
        in_hbm(out_grads.T),
        in_hbm(error.reshape(BLOCKS, block, cols)),
        in_hbm(query.T),
    )
    piece = scatter_sum(partial, XC)
    piece = scatter_sum(piece.reshape(8, rank // 8, LANES), Y)
    piece = gather_sum(piece, Z)
    piece = gather(piece, Y).reshape(rank, LANES)
    factor = lax.all_gather(gather(piece, "x"), "c", tiled=True)

    piece = scatter_sum(project(factor, merged), XYC)
    piece, factor = lax.optimization_barrier((piece, factor))
    inverse, weights = invert(factor, lax.axis_size((Z, *XYC)))
    left = spread(factor, weights, block)
    piece = gather_sum(piece, Z)
    piece, left = lax.optimization_barrier((piece, left))
    tiles = gather(piece, XYC)
    error_new, momentum_new, query_t = finish(
        inverse, tiles, left, merged, in_hbm(momentum.reshape(BLOCKS, block, cols))
    )
    return (error_new.reshape(error.shape), momentum_new.reshape(momentum.shape), query_t.T)


def solution(mesh):
    fine = Mesh(mesh.devices.reshape(12, 4, 2, 2, 4), ("z", "x", "yl", "c", "yh"))
    rep, shard = ("z", "x", "yl", "c"), "yh"
    return jax.shard_map(
        shards,
        mesh=fine,
        in_specs=(
            P(rep, None),
            P(rep, shard),
            P(rep, None, shard),
            P(None, shard),
            P(shard, None),
        ),
        out_specs=(P(rep, None, shard), P(None, shard), P(shard, None)),
        check_vma=False,
    )
```

```python
import functools
import itertools

import jax
import jax.numpy as jnp
from jax import lax
from jax.experimental import pallas as pl
from jax.experimental.pallas import tpu as pltpu
from jax.sharding import Mesh, PartitionSpec as P

F32, BF16 = jnp.float32, jnp.bfloat16
BLOCKS, GROUP, LANES = 8, 4, 256
XC = ("x", "c")
Y = ("yl", "yh")
XYC = ("x", "yl", "c")
Z = "z"
FIRST = {"z": 9, "x": 2, "yh": 2}
NN = (((1,), (0,)), ((), ()))
NT = (((1,), (1,)), ((), ()))
TN = (((0,), (0,)), ((), ()))


def in_hbm(value):
    return pltpu.with_memory_space_constraint(value, pltpu.HBM)


def params(mib):
    return pltpu.CompilerParams(vmem_limit_bytes=mib << 20)


def cost(flops, size):
    return pl.CostEstimate(flops=flops, bytes_accessed=size, transcendentals=0)


def split(value):
    high = value.astype(BF16)
    return high, (value - high.astype(F32)).astype(BF16)


def dot(left, right, dims):
    return lax.dot_general(left, right, dims, preferred_element_type=F32)


def dot_split(left, right, dims):
    (lh, ll), (rh, rl) = left, right
    return dot(lh, rh, dims) + (dot(lh, rl, dims) + dot(ll, rh, dims))


def dot_full(left, right, dims):
    return lax.dot_general(
        left, right, dims, precision=lax.Precision.HIGHEST, preferred_element_type=F32
    )


def merge_kernel(act_hbm, grad_hbm, err_hbm, query_hbm, merged_ref, partial_ref,
                 act_ref, grad_ref, err_ref, query_ref, sems):
    blocks, rows = merged_ref.shape[:2]
    rank = partial_ref.shape[1]
    small = [
        pltpu.make_async_copy(grad_hbm, grad_ref, sems.at[0]),
        pltpu.make_async_copy(query_hbm, query_ref, sems.at[1]),
    ]
    large = []
    for g in range(0, blocks, GROUP):
        part = pl.ds(g, GROUP)
        large.append([
            pltpu.make_async_copy(act_hbm.at[part], act_ref.at[part], sems.at[2 + g]),
            pltpu.make_async_copy(err_hbm.at[part], err_ref.at[part], sems.at[3 + g]),
        ])
    for copy in [*small, *sum(large, [])]:
        copy.start()
    partial_ref[:, :, rows:] = jnp.zeros((blocks, rank, LANES - rows), F32)
    for copy in small:
        copy.wait()
    stacked = jnp.concatenate(split(query_ref[...]), axis=0)
    grad_t = grad_ref[...].astype(F32).T.astype(BF16)
    for b in range(blocks):
        if b % GROUP == 0:
            for copy in large[b // GROUP]:
                copy.wait()
        merged = dot(act_ref[b], grad_t, NN) + err_ref[b].astype(F32)
        merged_ref[b] = merged
        high, low = split(merged)
        both = dot(stacked, high, NT)
        partial_ref[b, :, :rows] = both[:rank] + (both[rank:] + dot(stacked[:rank], low, NT))


def merge(act, grad, err, query):
    blocks, rows, cols = err.shape
    rank = query.shape[0]
    whole = pl.BlockSpec(memory_space=pltpu.VMEM)
    hbm = pl.BlockSpec(memory_space=pltpu.HBM)
    return pl.pallas_call(
        merge_kernel,
        in_specs=[hbm] * 4,
        out_specs=[whole] * 2,
        out_shape=[
            jax.ShapeDtypeStruct((blocks, rows, cols), F32),
            jax.ShapeDtypeStruct((blocks, rank, LANES), F32),
        ],
        scratch_shapes=[
            *(pltpu.VMEM(value.shape, value.dtype) for value in (act, grad, err, query)),
            pltpu.SemaphoreType.DMA((2 + blocks,)),
        ],
        compiler_params=params(16),
        cost_estimate=cost(500_000_000, 4 << 20),
        name="merge",
    )(act, grad, err, query)


def project_kernel(factor_ref, merged_ref, tiles_ref):
    blocks, rows, cols = merged_ref.shape
    rank = factor_ref.shape[1]
    both, rest = jnp.zeros((2 * rank, cols), F32), jnp.zeros((rank, cols), F32)
    for b in range(blocks):
        stacked = jnp.concatenate(split(factor_ref[b][:, :rows]), axis=0)
        high, low = split(merged_ref[b])
        both += dot(stacked, high, NN)
        rest += dot(stacked[:rank], low, NN)
    total = both[:rank] + (both[rank:] + rest)
    total = jnp.concatenate([total, jnp.zeros((rank, LANES - cols), F32)], axis=1)
    for j in range(tiles_ref.shape[0]):
        r, c = divmod(j, 2)
        tiles_ref[j] = total[8 * r : 8 * r + 8, 128 * c : 128 * c + 128]


def project(factor, merged):
    rank = factor.shape[1]
    whole = pl.BlockSpec(memory_space=pltpu.VMEM)
    return pl.pallas_call(
        project_kernel,
        in_specs=[whole] * 2,
        out_specs=whole,
        out_shape=jax.ShapeDtypeStruct((rank * LANES // 1024, 8, 128), F32),
        compiler_params=params(16),
        cost_estimate=cost(400_000_000, 3 << 20),
        name="project",
    )(factor, merged)


def invert_kernel(replicas, factor_ref, inverse_ref, weights_ref):
    blocks, rank = factor_ref.shape[:2]
    gram = jnp.zeros((rank, rank), F32)
    for b in range(blocks):
        gram += dot_full(factor_ref[b], factor_ref[b], NT)
    lane = lax.broadcasted_iota(jnp.int32, (rank, rank), 1)
    eye = (lane == lax.broadcasted_iota(jnp.int32, (rank, rank), 0)).astype(F32)
    wide = jnp.concatenate([gram, eye], axis=1)
    tiles = [wide[8 * t : 8 * t + 8] for t in range(rank // 8)]
    sub = lax.broadcasted_iota(jnp.int32, (8, 1), 0)
    for k in range(rank):
        at, r = divmod(k, 8)
        row = tiles[at][r : r + 1]
        scaled = row * (1.0 / row[:, k : k + 1])
        for t in range(at, len(tiles)):
            column = tiles[t][:, k : k + 1]
            if t == at and r == 7:
                continue
            if t == at:
                column = jnp.where(sub > r, column, 0.0)
            tiles[t] = tiles[t] - column * scaled
    wide = jnp.concatenate(tiles, axis=0)
    pivots = jnp.sum(wide[:, :rank] * eye, axis=1, keepdims=True)
    inverse = wide[:, rank:] / jnp.sqrt(pivots)
    inverse_ref[...] = inverse / replicas
    weights_ref[...] = dot_full(inverse, inverse, TN) / replicas


def invert(factor, replicas):
    rank = factor.shape[1]
    square = jax.ShapeDtypeStruct((rank, rank), F32)
    return pl.pallas_call(
        lambda *refs: invert_kernel(replicas, *refs),
        out_shape=[square, square],
        compiler_params=params(16),
        cost_estimate=cost(7_000_000_000, 1 << 20),
        name="invert",
    )(factor)


def spread_kernel(factor_ref, weights_ref, left_ref):
    blocks, rows = left_ref.shape[:2]
    for b in range(blocks):
        left = split(dot_full(weights_ref[...], factor_ref[b], TN).T[:rows])
        left_ref[b] = jnp.concatenate(left, axis=1)


def spread(factor, weights, rows):
    blocks, rank = factor.shape[:2]
    return pl.pallas_call(
        spread_kernel,
        out_shape=jax.ShapeDtypeStruct((blocks, rows, 2 * rank), BF16),
        compiler_params=params(16),
        cost_estimate=cost(2_000_000_000, 1 << 20),
        name="spread",
    )(factor, weights)


def finish_kernel(inverse_ref, tiles_ref, left_ref, merged_ref, mom_hbm,
                  error_hbm, momentum_hbm, query_ref, mom_ref, error_ref, momentum_ref, approx_ref, sems):
    rank, cols = query_ref.shape
    blocks, rows = merged_ref.shape[:2]
    loads, stores = [], []
    for g in range(0, blocks, GROUP):
        part = pl.ds(g, GROUP)
        loads.append(pltpu.make_async_copy(mom_hbm.at[part], mom_ref.at[part], sems.at[0, g // GROUP]))
        stores.append([
            pltpu.make_async_copy(error_ref.at[part], error_hbm.at[part], sems.at[1, g // GROUP]),
            pltpu.make_async_copy(momentum_ref.at[part], momentum_hbm.at[part], sems.at[2, g // GROUP]),
        ])
    for copy in loads:
        copy.start()
    total = jnp.concatenate(
        [
            jnp.concatenate([tiles_ref[j], tiles_ref[j + 1]], axis=1)
            for j in range(0, tiles_ref.shape[0], 2)
        ],
        axis=0,
    )
    high, low = split(total)
    right = jnp.concatenate([high, high, low], axis=0)
    for b in range(blocks):
        left = left_ref[b]
        left = jnp.concatenate([left, left[:, :rank]], axis=1)
        approx = dot(left, right, NN)[:, :cols]
        approx_ref[b] = approx
        error_ref[b] = (merged_ref[b] - approx).astype(BF16)
        if b % GROUP == GROUP - 1:
            stores[b // GROUP][0].start()
    for b in range(blocks):
        if b % GROUP == 0:
            loads[b // GROUP].wait()
        momentum_ref[b] = (0.9 * mom_ref[b].astype(F32) + approx_ref[b]).astype(BF16)
        if b % GROUP == GROUP - 1:
            stores[b // GROUP][1].start()
    query_ref[...] = dot_full(inverse_ref[...], total, NN)[:, :cols]
    for pair in stores:
        for copy in pair:
            copy.wait()


def finish(inverse, tiles, left, merged, momentum):
    blocks, rows, cols = merged.shape
    rank = inverse.shape[0]
    whole = pl.BlockSpec(memory_space=pltpu.VMEM)
    hbm = pl.BlockSpec(memory_space=pltpu.HBM)
    out = jax.ShapeDtypeStruct((blocks, rows, cols), BF16)
    return pl.pallas_call(
        finish_kernel,
        in_specs=[whole, whole, whole, whole, hbm],
        out_specs=[hbm, hbm, whole],
        out_shape=[out, out, jax.ShapeDtypeStruct((rank, cols), F32)],
        scratch_shapes=[
            *(pltpu.VMEM((blocks, rows, cols), BF16) for _ in range(3)),
            pltpu.VMEM((blocks, rows, cols), F32),
            pltpu.SemaphoreType.DMA((3, blocks // GROUP)),
        ],
        compiler_params=params(16),
        cost_estimate=cost(400_000_000, 6 << 20),
        name="finish",
    )(inverse, tiles, left, merged, momentum)


def group_of(axes):
    names = axes if isinstance(axes, tuple) else (axes,)
    sizes = [lax.axis_size(name) for name in names]
    first = [FIRST.get(name, 0) for name in names]
    order = [
        [(f + i) % n for f, i, n in zip(first, index, sizes)]
        for index in itertools.product(*(range(n) for n in sizes))
    ]
    if names == XC:
        order.sort(key=lambda at: at[1])
    return [[functools.reduce(lambda a, v: a * v[1] + v[0], zip(at, sizes), 0) for at in order]]


def exchange(pieces, axes):
    return lax.all_to_all(pieces, axes, 0, 0, axis_index_groups=group_of(axes))


def scatter_sum(pieces, axes):
    return jnp.sum(exchange(pieces, axes), 0)


def gather(piece, axes):
    copies = jnp.broadcast_to(piece[None], (lax.axis_size(axes), *piece.shape))
    return exchange(copies, axes)


def gather_sum(piece, axes):
    return jnp.sum(gather(piece, axes), 0)


def shards(activations, out_grads, error, momentum, query):
    rows, cols = error.shape[1:]
    rank = query.shape[1]
    block = rows // BLOCKS
    merged, partial = merge(
        in_hbm(activations.T.reshape(BLOCKS, block, -1)),
        in_hbm(out_grads.T),
        in_hbm(error.reshape(BLOCKS, block, cols)),
        in_hbm(query.T),
    )
    piece = scatter_sum(partial, XC)
    piece = scatter_sum(piece.reshape(8, rank // 8, LANES), Y)
    piece = gather_sum(piece, Z)
    piece = gather(piece, Y).reshape(rank, LANES)
    factor = lax.all_gather(gather(piece, "x"), "c", tiled=True)

    piece = scatter_sum(project(factor, merged), XYC)
    piece, factor = lax.optimization_barrier((piece, factor))
    inverse, weights = invert(factor, lax.axis_size((Z, *XYC)))
    left = spread(factor, weights, block)
    piece = gather_sum(piece, Z)
    piece, left = lax.optimization_barrier((piece, left))
    tiles = gather(piece, XYC)
    error_new, momentum_new, query_t = finish(
        inverse, tiles, left, merged, in_hbm(momentum.reshape(BLOCKS, block, cols))
    )
    return (error_new.reshape(error.shape), momentum_new.reshape(momentum.shape), query_t.T)


def solution(mesh):
    fine = Mesh(mesh.devices.reshape(12, 4, 2, 2, 4), ("z", "x", "yl", "c", "yh"))
    rep, shard = ("z", "x", "yl", "c"), "yh"
    return jax.shard_map(
        shards,
        mesh=fine,
        in_specs=(
            P(rep, None),
            P(rep, shard),
            P(rep, None, shard),
            P(None, shard),
            P(shard, None),
        ),
        out_specs=(P(rep, None, shard), P(None, shard), P(shard, None)),
        check_vma=False,
    )
```

```python
import functools
import itertools

import jax
import jax.numpy as jnp
from jax import lax
from jax.experimental import pallas as pl
from jax.experimental.pallas import tpu as pltpu
from jax.sharding import Mesh, PartitionSpec as P

F32, BF16 = jnp.float32, jnp.bfloat16
BLOCKS, GROUP, LANES = 8, 4, 256
XC = ("x", "c")
Y = ("yl", "yh")
XYC = ("x", "yl", "c")
Z = "z"
FIRST = {"z": 9, "x": 2, "yh": 2}
NN = (((1,), (0,)), ((), ()))
NT = (((1,), (1,)), ((), ()))
TN = (((0,), (0,)), ((), ()))


def in_hbm(value):
    return pltpu.with_memory_space_constraint(value, pltpu.HBM)


def params(mib):
    return pltpu.CompilerParams(vmem_limit_bytes=mib << 20)


def cost(flops, size):
    return pl.CostEstimate(flops=flops, bytes_accessed=size, transcendentals=0)


def split(value):
    high = value.astype(BF16)
    return high, (value - high.astype(F32)).astype(BF16)


def dot(left, right, dims):
    return lax.dot_general(left, right, dims, preferred_element_type=F32)


def dot_split(left, right, dims):
    (lh, ll), (rh, rl) = left, right
    return dot(lh, rh, dims) + (dot(lh, rl, dims) + dot(ll, rh, dims))


def dot_full(left, right, dims):
    return lax.dot_general(
        left, right, dims, precision=lax.Precision.HIGHEST, preferred_element_type=F32
    )


def merge_kernel(act_hbm, grad_hbm, err_hbm, query_hbm, merged_ref, partial_ref,
                 act_ref, grad_ref, err_ref, query_ref, sems):
    blocks, rows = merged_ref.shape[:2]
    rank = partial_ref.shape[1]
    small = [
        pltpu.make_async_copy(grad_hbm, grad_ref, sems.at[0]),
        pltpu.make_async_copy(query_hbm, query_ref, sems.at[1]),
    ]
    large = []
    for g in range(0, blocks, GROUP):
        part = pl.ds(g, GROUP)
        large.append([
            pltpu.make_async_copy(act_hbm.at[part], act_ref.at[part], sems.at[2 + g]),
            pltpu.make_async_copy(err_hbm.at[part], err_ref.at[part], sems.at[3 + g]),
        ])
    for copy in [*small, *sum(large, [])]:
        copy.start()
    partial_ref[:, :, rows:] = jnp.zeros((blocks, rank, LANES - rows), F32)
    for copy in small:
        copy.wait()
    stacked = jnp.concatenate(split(query_ref[...]), axis=0)
    grad_t = grad_ref[...].astype(F32).T.astype(BF16)
    for b in range(blocks):
        if b % GROUP == 0:
            for copy in large[b // GROUP]:
                copy.wait()
        merged = dot(act_ref[b], grad_t, NN) + err_ref[b].astype(F32)
        merged_ref[b] = merged
        high, low = split(merged)
        both = dot(stacked, high, NT)
        partial_ref[b, :, :rows] = both[:rank] + (both[rank:] + dot(stacked[:rank], low, NT))


def merge(act, grad, err, query):
    blocks, rows, cols = err.shape
    rank = query.shape[0]
    whole = pl.BlockSpec(memory_space=pltpu.VMEM)
    hbm = pl.BlockSpec(memory_space=pltpu.HBM)
    return pl.pallas_call(
        merge_kernel,
        in_specs=[hbm] * 4,
        out_specs=[whole] * 2,
        out_shape=[
            jax.ShapeDtypeStruct((blocks, rows, cols), F32),
            jax.ShapeDtypeStruct((blocks, rank, LANES), F32),
        ],
        scratch_shapes=[
            *(pltpu.VMEM(value.shape, value.dtype) for value in (act, grad, err, query)),
            pltpu.SemaphoreType.DMA((2 + blocks,)),
        ],
        compiler_params=params(16),
        cost_estimate=cost(500_000_000, 4 << 20),
        name="merge",
    )(act, grad, err, query)


def project_kernel(factor_ref, merged_ref, tiles_ref):
    blocks, rows, cols = merged_ref.shape
    rank = factor_ref.shape[1]
    both, rest = jnp.zeros((2 * rank, cols), F32), jnp.zeros((rank, cols), F32)
    for b in range(blocks):
        stacked = jnp.concatenate(split(factor_ref[b][:, :rows]), axis=0)
        high, low = split(merged_ref[b])
        both += dot(stacked, high, NN)
        rest += dot(stacked[:rank], low, NN)
    total = both[:rank] + (both[rank:] + rest)
    total = jnp.concatenate([total, jnp.zeros((rank, LANES - cols), F32)], axis=1)
    for j in range(tiles_ref.shape[0]):
        r, c = divmod(j, 2)
        tiles_ref[j] = total[8 * r : 8 * r + 8, 128 * c : 128 * c + 128]


def project(factor, merged):
    rank = factor.shape[1]
    whole = pl.BlockSpec(memory_space=pltpu.VMEM)
    return pl.pallas_call(
        project_kernel,
        in_specs=[whole] * 2,
        out_specs=whole,
        out_shape=jax.ShapeDtypeStruct((rank * LANES // 1024, 8, 128), F32),
        compiler_params=params(16),
        cost_estimate=cost(400_000_000, 3 << 20),
        name="project",
    )(factor, merged)


def invert_kernel(replicas, factor_ref, inverse_ref, weights_ref):
    blocks, rank = factor_ref.shape[:2]
    gram = jnp.zeros((rank, rank), F32)
    for b in range(blocks):
        gram += dot_full(factor_ref[b], factor_ref[b], NT)
    lane = lax.broadcasted_iota(jnp.int32, (rank, rank), 1)
    eye = (lane == lax.broadcasted_iota(jnp.int32, (rank, rank), 0)).astype(F32)
    wide = jnp.concatenate([gram, eye], axis=1)
    tiles = [wide[8 * t : 8 * t + 8] for t in range(rank // 8)]
    sub = lax.broadcasted_iota(jnp.int32, (8, 1), 0)
    for k in range(rank):
        at, r = divmod(k, 8)
        row = tiles[at][r : r + 1]
        scaled = row * (1.0 / row[:, k : k + 1])
        for t in range(at, len(tiles)):
            column = tiles[t][:, k : k + 1]
            if t == at and r == 7:
                continue
            if t == at:
                column = jnp.where(sub > r, column, 0.0)
            tiles[t] = tiles[t] - column * scaled
    wide = jnp.concatenate(tiles, axis=0)
    pivots = jnp.sum(wide[:, :rank] * eye, axis=1, keepdims=True)
    inverse = wide[:, rank:] / jnp.sqrt(pivots)
    inverse_ref[...] = inverse / replicas
    weights_ref[...] = dot_full(inverse, inverse, TN) / replicas


def invert(factor, replicas):
    rank = factor.shape[1]
    square = jax.ShapeDtypeStruct((rank, rank), F32)
    return pl.pallas_call(
        lambda *refs: invert_kernel(replicas, *refs),
        out_shape=[square, square],
        compiler_params=params(16),
        cost_estimate=cost(7_000_000_000, 1 << 20),
        name="invert",
    )(factor)


def spread_kernel(factor_ref, weights_ref, left_ref):
    blocks, rows = left_ref.shape[:2]
    for b in range(blocks):
        left = split(dot_full(weights_ref[...], factor_ref[b], TN).T[:rows])
        left_ref[b] = jnp.concatenate(left, axis=1)


def spread(factor, weights, rows):
    blocks, rank = factor.shape[:2]
    return pl.pallas_call(
        spread_kernel,
        out_shape=jax.ShapeDtypeStruct((blocks, rows, 2 * rank), BF16),
        compiler_params=params(16),
        cost_estimate=cost(2_000_000_000, 1 << 20),
        name="spread",
    )(factor, weights)


def finish_kernel(inverse_ref, tiles_ref, left_ref, merged_ref, mom_hbm,
                  error_hbm, momentum_hbm, query_ref, mom_ref, error_ref, momentum_ref, approx_ref, sems):
    rank, cols = query_ref.shape
    blocks, rows = merged_ref.shape[:2]
    loads, stores = [], []
    for g in range(0, blocks, GROUP):
        part = pl.ds(g, GROUP)
        loads.append(pltpu.make_async_copy(mom_hbm.at[part], mom_ref.at[part], sems.at[0, g // GROUP]))
        stores.append([
            pltpu.make_async_copy(error_ref.at[part], error_hbm.at[part], sems.at[1, g // GROUP]),
            pltpu.make_async_copy(momentum_ref.at[part], momentum_hbm.at[part], sems.at[2, g // GROUP]),
        ])
    for copy in loads:
        copy.start()
    total = jnp.concatenate(
        [
            jnp.concatenate([tiles_ref[j], tiles_ref[j + 1]], axis=1)
            for j in range(0, tiles_ref.shape[0], 2)
        ],
        axis=0,
    )
    high, low = split(total)
    right = jnp.concatenate([high, high, low], axis=0)
    for b in range(blocks):
        left = left_ref[b]
        left = jnp.concatenate([left, left[:, :rank]], axis=1)
        approx = dot(left, right, NN)[:, :cols]
        approx_ref[b] = approx
        error_ref[b] = (merged_ref[b] - approx).astype(BF16)
        if b % GROUP == GROUP - 1:
            stores[b // GROUP][0].start()
    for b in range(blocks):
        if b % GROUP == 0:
            loads[b // GROUP].wait()
        momentum_ref[b] = (0.9 * mom_ref[b].astype(F32) + approx_ref[b]).astype(BF16)
        if b % GROUP == GROUP - 1:
            stores[b // GROUP][1].start()
    query_ref[...] = dot_full(inverse_ref[...], total, NN)[:, :cols]
    for pair in stores:
        for copy in pair:
            copy.wait()


def finish(inverse, tiles, left, merged, momentum):
    blocks, rows, cols = merged.shape
    rank = inverse.shape[0]
    whole = pl.BlockSpec(memory_space=pltpu.VMEM)
    hbm = pl.BlockSpec(memory_space=pltpu.HBM)
    out = jax.ShapeDtypeStruct((blocks, rows, cols), BF16)
    return pl.pallas_call(
        finish_kernel,
        in_specs=[whole, whole, whole, whole, hbm],
        out_specs=[hbm, hbm, whole],
        out_shape=[out, out, jax.ShapeDtypeStruct((rank, cols), F32)],
        scratch_shapes=[
            *(pltpu.VMEM((blocks, rows, cols), BF16) for _ in range(3)),
            pltpu.VMEM((blocks, rows, cols), F32),
            pltpu.SemaphoreType.DMA((3, blocks // GROUP)),
        ],
        compiler_params=params(16),
        cost_estimate=cost(400_000_000, 6 << 20),
        name="finish",
    )(inverse, tiles, left, merged, momentum)


def group_of(axes):
    names = axes if isinstance(axes, tuple) else (axes,)
    sizes = [lax.axis_size(name) for name in names]
    first = [FIRST.get(name, 0) for name in names]
    if names == XYC:
        first[1] = 1
    order = [
        [(f + i) % n for f, i, n in zip(first, index, sizes)]
        for index in itertools.product(*(range(n) for n in sizes))
    ]
    if names == XC:
        order.sort(key=lambda at: at[1])
    return [[functools.reduce(lambda a, v: a * v[1] + v[0], zip(at, sizes), 0) for at in order]]


def exchange(pieces, axes):
    return lax.all_to_all(pieces, axes, 0, 0, axis_index_groups=group_of(axes))


def scatter_sum(pieces, axes):
    return jnp.sum(exchange(pieces, axes), 0)


def gather(piece, axes):
    copies = jnp.broadcast_to(piece[None], (lax.axis_size(axes), *piece.shape))
    return exchange(copies, axes)


def gather_sum(piece, axes):
    return jnp.sum(gather(piece, axes), 0)


def shards(activations, out_grads, error, momentum, query):
    rows, cols = error.shape[1:]
    rank = query.shape[1]
    block = rows // BLOCKS
    merged, partial = merge(
        in_hbm(activations.T.reshape(BLOCKS, block, -1)),
        in_hbm(out_grads.T),
        in_hbm(error.reshape(BLOCKS, block, cols)),
        in_hbm(query.T),
    )
    piece = scatter_sum(partial, XC)
    piece = scatter_sum(piece.reshape(8, rank // 8, LANES), Y)
    piece = gather_sum(piece, Z)
    piece = gather(piece, Y).reshape(rank, LANES)
    factor = lax.all_gather(gather(piece, "x"), "c", tiled=True)

    piece = scatter_sum(project(factor, merged), XYC)
    piece, factor = lax.optimization_barrier((piece, factor))
    inverse, weights = invert(factor, lax.axis_size((Z, *XYC)))
    left = spread(factor, weights, block)
    piece = gather_sum(piece, Z)
    piece, left = lax.optimization_barrier((piece, left))
    tiles = gather(piece, XYC)
    error_new, momentum_new, query_t = finish(
        inverse, tiles, left, merged, in_hbm(momentum.reshape(BLOCKS, block, cols))
    )
    return (error_new.reshape(error.shape), momentum_new.reshape(momentum.shape), query_t.T)


def solution(mesh):
    fine = Mesh(mesh.devices.reshape(12, 4, 2, 2, 4), ("z", "x", "yl", "c", "yh"))
    rep, shard = ("z", "x", "yl", "c"), "yh"
    return jax.shard_map(
        shards,
        mesh=fine,
        in_specs=(
            P(rep, None),
            P(rep, shard),
            P(rep, None, shard),
            P(None, shard),
            P(shard, None),
        ),
        out_specs=(P(rep, None, shard), P(None, shard), P(shard, None)),
        check_vma=False,
    )
```
